32 devices in a mesh: seq: 16 (over z, y, x), chan: 2 (over core).
Axes of the slice: x: 2, y: 2, z: 4, core: 2. Of those that a mesh axis runs over, the one named last changes fastest.
Arguments:
- streams: bfloat16 [3, 4096, 2048], P(None, 'chan', 'seq'), may hold values from -16 to 16
- feat_weights: float32 [3, 4096, 3], P(None, 'chan'), may hold values from -3.5 to 3.5
- skip_gain: float32 [4096], P('chan'), may hold values from -4 to 4
- filter_taps: bfloat16 [4096, 2048], P('chan', 'seq'), may hold values from -2 to 2
Outputs:
- normed_out: bfloat16 [4096, 2048], P('chan', 'seq')
The draws below stay inside these ranges and needn't reach their ends.
All inputs are finite; a program needn't handle non-finite values.
Results may differ from the reference program's by a relative error of at most 0.0075.
Values may be sent and summed in bfloat16 or wider, within the bound.
A program may use at most 64 MiB of HBM per device.

```python
import math
import jax
import jax.numpy as jnp
from jax import lax

C = 4096
TAPS = 3
L = 2048


def draw_streams(key, part):
    key_base = jax.random.fold_in(key, 0)
    channel_pos = jnp.arange(C, dtype=jnp.float32)
    q_scale = 0.3 * jnp.power(10.0, channel_pos / C)
    base = jnp.clip(jax.random.normal(key_base, (3, C, L), jnp.float32), -4.0, 4.0)
    scales = jnp.concatenate([q_scale[None, :], jnp.ones((2, C), jnp.float32)], axis=0)
    return (base * scales[:, :, None]).astype(jnp.bfloat16)


def draw_filter_taps(key, part):
    key_pick, key_slow, key_fast, key_taps = jax.random.split(key, 4)
    slow_share = 0.5
    slow_pick = jax.random.uniform(key_pick, (C, 1), jnp.float32) < slow_share
    tau_slow = jnp.exp(jax.random.uniform(key_slow, (C, 1), jnp.float32, math.log(L / 2.0), math.log(8.0 * L)))
    tau_fast = jnp.exp(jax.random.uniform(key_fast, (C, 1), jnp.float32, math.log(8.0), math.log(40.0)))
    head_weight = jnp.where(slow_pick, 0.0, math.sqrt(0.7))
    tail_weight = jnp.where(slow_pick, 1.0, math.sqrt(0.3))
    lags = jnp.arange(L, dtype=jnp.float32)[None, :]
    head_part = head_weight * jnp.sqrt(2.0 / tau_fast) * jnp.exp(-lags / tau_fast)
    tail_part = tail_weight * jnp.sqrt(2.0 / jnp.minimum(tau_slow, float(L))) * jnp.exp(-lags / tau_slow)
    rough = jnp.clip(jax.random.normal(key_taps, (C, L), jnp.float32), -4.0, 4.0)
    return (rough * (head_part + tail_part)).astype(jnp.bfloat16)


def block_levels(own_key, extent, cuts, smallest, top_value):
    factor_of, own = 1.0, jax.random.fold_in(own_key, 6)
    for dim, shards_of in cuts:
        heights = jnp.exp(jax.random.uniform(jax.random.fold_in(own, dim), (shards_of,), jnp.float32, smallest / len(cuts), top_value / len(cuts)))
        factor_of = factor_of * jnp.repeat(heights, extent[dim] // shards_of).reshape([-1 if axis == dim else 1 for axis in range(len(extent))])
    return factor_of


def centred(own_key, extent, spread, reach, cuts=(), held_as=jnp.bfloat16):
    drawn = jax.random.normal(own_key, extent, jnp.float32) * spread
    if len(cuts) > 0:
        drawn = block_levels(own_key, extent, cuts, -0.22, 0.18) * drawn
    return jnp.clip(drawn, min=-reach, max=reach).astype(held_as)


def setup_inputs(seed: int = 0) -> dict:
    keys = jax.random.split(jax.random.key(seed), 5)
    streams = draw_streams(jax.random.fold_in(keys[4], 71), 0)
    feat_weights = centred(keys[1], (3, C, TAPS), TAPS ** -0.5, 3.5, ((1, 2),), jnp.float32)
    skip_gain = centred(keys[2], (C,), 1.0, 4.0, ((0, 2),), jnp.float32)
    filter_taps = draw_filter_taps(jax.random.fold_in(keys[4], 71), 0)
    return dict(streams=streams, feat_weights=feat_weights, skip_gain=skip_gain, filter_taps=filter_taps)


EPS = 1e-05

def short_conv(slab_part, weights):
    length = slab_part.shape[2]
    padded = jnp.pad(slab_part, ((0, 0), (0, 0), (TAPS - 1, 0)))
    result = jnp.zeros_like(slab_part)
    for offset in range(TAPS):
        begin = TAPS - 1 - offset
        result = result + weights[:, :, offset:offset + 1] * padded[:, :, begin:begin + length]
    return result

def reference(streams, feat_weights, skip_gain, filter_taps):
    block_len = math.gcd(C, 32)

    def one_block(block_idx):
        start_at = (block_idx * block_len).astype(jnp.int32)
        slab_part = lax.dynamic_slice_in_dim(streams, start_at, block_len, 1).astype(jnp.float32)
        weights = lax.dynamic_slice_in_dim(feat_weights, start_at, block_len, 1)
        filter_part = lax.dynamic_slice_in_dim(filter_taps, start_at, block_len, 0).astype(jnp.float32)
        skip_part = lax.dynamic_slice_in_dim(skip_gain, start_at, block_len, 0)
        featured = short_conv(slab_part, weights)
        gated_vals = (featured[1] * featured[2]).astype(jnp.bfloat16)
        gated_float = gated_vals.astype(jnp.float32)
        spectrum_prod = jnp.fft.rfft(gated_float, n=2 * L, axis=-1) * jnp.fft.rfft(filter_part, n=2 * L, axis=-1)
        convolved = jnp.fft.irfft(spectrum_prod, n=2 * L, axis=-1)[:, :L]
        return featured[0] * (convolved + skip_part[:, None] * gated_float)
    mixed_out = lax.map(one_block, jnp.arange(C // block_len, dtype=jnp.int32)).reshape(C, L)
    totals = lax.optimization_barrier(jnp.sum(mixed_out * mixed_out, axis=0))
    inv_rms = lax.rsqrt(totals / C + EPS)
    return (mixed_out * inv_rms[None, :]).astype(jnp.bfloat16)
```

```python
import functools
import math

import jax
import jax.numpy as jnp
import numpy as np
from jax import lax
from jax.experimental import pallas as pl
from jax.experimental.pallas import tpu as pltpu
from jax.sharding import PartitionSpec as P

C = 4096
TAPS = 3
EPS = 1e-05


def add(a, b):
    if a is None:
        return b
    return a if b is None else a + b


def sub(a, b):
    if b is None:
        return a
    return -b if a is None else a - b


def times(pair, angle):
    re, im = pair
    c, s = math.cos(angle), math.sin(angle)
    if abs(s) < 1e-12 and c > 0:
        return pair
    if abs(c) < 1e-12:
        turned = (None if im is None else -im, re)
        return turned if s > 0 else (None if turned[0] is None else -turned[0], -re)
    if im is None:
        return (re * c, re * s)
    return (re * c - im * s, re * s + im * c)


def real_fft(xs, n):
    if n == 2:
        return [(xs[0], None), (xs[0], None)]
    even = real_fft(xs[0::2], n // 2)
    odd = real_fft(xs[1::2], n // 2)
    out = [None] * (n // 2 + 1)
    for k in range(n // 4 + 1):
        er, ei = even[k]
        tr, ti = times(odd[k], -2.0 * math.pi * k / n)
        out[k] = (add(er, tr), add(ei, ti))
        if n // 2 - k != k:
            out[n // 2 - k] = (sub(er, tr), sub(ti, ei))
    return out


def real_ifft(spec, n):
    if n == 2:
        return [spec[0][0] + spec[1][0]]
    even, odd = [], []
    for k in range(n // 4 + 1):
        ar, ai = spec[k]
        br, bi = spec[n // 2 - k]
        if n // 2 - k == k:
            er, ei, dr, di = ar + ar, None, None, add(ai, ai)
            even.append((er, ei))
            odd.append((-di if di is not None else None, None))
            continue
        even.append((ar + br, sub(ai, bi)))
        odd.append(times((ar - br, add(ai, bi)), 2.0 * math.pi * k / n))
    first = real_ifft(even, n // 2)
    second = real_ifft(odd, n // 2)
    out = []
    for a, b in zip(first, second):
        out += [a, b]
    return out


def tables(blocks, width):
    total = 2 * blocks * width
    k1 = np.arange(blocks + 1)[:, None]
    i = np.arange(width)[None, :]
    ang = 2.0 * np.pi * ((k1 * i) % total) / total
    twist = np.stack([np.cos(ang), np.sin(ang)]).astype(np.float32)[:, :, None, :]
    j = np.arange(width)
    ang = 2.0 * np.pi * ((j[:, None] * j[None, :]) % width) / width
    c, s = np.cos(ang), np.sin(ang)
    forward = np.block([[c, -s], [s, c]])
    inverse = np.block([[c, s], [-s, c]]) / total
    out = []
    for m in (forward, inverse):
        hi = m.astype(np.float32).astype(jnp.bfloat16)
        lo = (m - hi.astype(np.float64)).astype(np.float32).astype(jnp.bfloat16)
        out += [hi, lo]
    return twist, np.stack(out)


def split_dot(x, hi_w, lo_w):
    hi = x.astype(jnp.bfloat16)
    lo = (x - hi.astype(jnp.float32)).astype(jnp.bfloat16)
    dot = functools.partial(jnp.dot, preferred_element_type=jnp.float32)
    return dot(hi, hi_w) + (dot(lo, hi_w) + dot(hi, lo_w))


def forward(load, twist, mats, buf, blocks, rows, width):
    stride = (twist.shape[1] - 1) // blocks
    xs = [load(a).astype(jnp.float32) for a in range(blocks)]
    for k, (re, im) in enumerate(real_fft(xs, 2 * blocks)):
        tc, ts = twist[0, k * stride], twist[1, k * stride]
        if k == 0:
            new_re, new_im = re, jnp.zeros_like(re)
        elif im is None:
            new_re, new_im = re * tc, -(re * ts)
        else:
            new_re, new_im = re * tc + im * ts, im * tc - re * ts
        buf[k, :, :width] = new_re
        buf[k, :, width:] = new_im
    flat = (blocks + 1) * rows
    return split_dot(buf[: blocks + 1].reshape(flat, 2 * width), mats[0], mats[1])


def backward(prod, store, twist, mats, buf, blocks, rows, width):
    back = split_dot(prod, mats[2], mats[3])
    buf[: blocks + 1] = back.reshape(blocks + 1, rows, 2 * width)
    stride = (twist.shape[1] - 1) // blocks
    spec = []
    for k in range(blocks + 1):
        re, im = buf[k, :, :width], buf[k, :, width:]
        tc, ts = twist[0, k * stride], twist[1, k * stride]
        out_re = re if k == 0 else re * tc - im * ts
        out_im = None if k in (0, blocks) else re * ts + im * tc
        spec.append((out_re, out_im))
    for a, y in enumerate(real_ifft(spec, 2 * blocks)):
        store(a, y.astype(jnp.bfloat16))


def column(cols, j):
    return cols[:, j : j + 1]


def fused_kernel(
    chunks, s_hbm, w_hbm, g_hbm, h_ref, twist_hbm, mats_hbm, out_ref,
    s_ref, w_ref, g_ref, twist, mats, halo_out, halo_in, cols_buf, gated, f0_buf, mix_buf, h_in, x_in, y_out, y_in,
    sum_out, sum_in, spec_buf, filt_buf,
    halo_sem, h_send, h_recv, x_send, x_recv, y_send, y_recv, sum_send, sum_recv, own_sem,
    load_sem,
):
    n, group, width = gated.shape
    part = group // chunks
    rows = math.gcd(part, 32)
    chans = n * group
    cores = sum_in.shape[0]
    me = lax.axis_index("seq")
    core = lax.axis_index("chan")
    mesh_id = pl.DeviceIdType.MESH

    loads = [
        pltpu.make_async_copy(src, dst, load_sem.at[i])
        for i, (src, dst) in enumerate(
            [(s_hbm, s_ref), (w_hbm, w_ref), (g_hbm, g_ref), (twist_hbm, twist), (mats_hbm, mats)]
        )
    ]
    for copy in loads:
        copy.start()

    barrier = pltpu.get_barrier_semaphore()

    def greet(o, carry):
        peer = lax.rem(me + o, n)
        pl.semaphore_signal(barrier, inc=1, device_id={"seq": peer}, device_id_type=mesh_id)
        return carry

    lax.fori_loop(1, n, greet, 0)
    for o in range(1, cores):
        pl.semaphore_signal(
            barrier, inc=1, device_id={"chan": lax.rem(core + o, cores)}, device_id_type=mesh_id
        )

    def sent(src, dst, send, recv, o, span):
        peer = lax.rem(me + o, n)
        return pltpu.make_async_remote_copy(
            src_ref=src.at[peer, span], dst_ref=dst.at[me, span],
            send_sem=send, recv_sem=recv,
            device_id={"seq": peer}, device_id_type=mesh_id,
        )

    everything = pl.ds(0, group)

    def send_h(o):
        return sent(h_ref, h_in, h_send.at[o], h_recv.at[o], o, everything)

    def send_x(o):
        return sent(gated, x_in, x_send.at[o], x_recv.at[o], o, everything)

    def start_all(make, first, end):
        def body(o, carry):
            make(o).start()
            return carry

        lax.fori_loop(first, end, body, 0)

    row = lax.broadcasted_iota(jnp.int32, (16, width), 0)
    lane = lax.broadcasted_iota(jnp.int32, (16, width), 1)
    last = None
    pl.semaphore_wait(barrier, n - 1 + cores - 1)
    start_all(send_h, 1, 1 + n // 2)
    loads[0].wait()
    for s in range(3):
        pick = ((row == 10 + 2 * s) & (lane == width - 2)) | (
            (row == 11 + 2 * s) & (lane == width - 1)
        )
        got = lax.dot_general(
            jnp.where(pick, 1.0, 0.0).astype(jnp.bfloat16),
            s_ref[s],
            (((1,), (1,)), ((), ())),
            preferred_element_type=jnp.float32,
        )
        last = got if last is None else last + got
    halo_out[...] = last.astype(jnp.bfloat16)

    halo = pltpu.make_async_remote_copy(
        src_ref=halo_out, dst_ref=halo_in, send_sem=halo_sem.at[0], recv_sem=halo_sem.at[1],
        device_id={"seq": lax.rem(me + 1, n)}, device_id_type=mesh_id,
    )
    halo.start()

    start_all(send_h, 1 + n // 2, n)
    own_h = pltpu.make_async_copy(h_ref.at[me], h_in.at[me], own_sem.at[0])
    own_h.start()
    loads[1].wait()
    loads[2].wait()
    halo.wait()
    for s in range(3):
        cols_buf[3 * s : 3 * s + 3, :] = w_ref[s]
    cols_buf[9:10, :] = g_ref[...]
    cols_buf[10:16, :] = jnp.where(me > 0, halo_in[...].astype(jnp.float32)[10:16], 0.0)

    tall = math.gcd(chans, 256)
    per = tall // group if tall > group else 1
    steps = chans // tall
    sub = tall
    lanes = lax.broadcasted_iota(jnp.int32, (sub, width), 1)

    source = lax.broadcasted_iota(jnp.int32, (width, 2 * width), 0)
    target = lax.broadcasted_iota(jnp.int32, (width, 2 * width), 1)
    moves = (target == source + 1) & (target < width)
    moves = moves | (target == source + width + 2)
    shift = jnp.where(moves, 1.0, 0.0).astype(jnp.bfloat16)

    def feature(step, carry):
        block = lax.rem(me // per + step, steps)
        begin = pl.multiple_of(block * tall, tall)
        columns = cols_buf[:, pl.ds(begin, tall)].T
        parts = []
        for r in range(0, tall, sub):
            cols = columns[r : r + sub]
            here = pl.ds(begin + r, sub)
            made = []
            for s in range(3):
                x = s_ref[s, here, :].astype(jnp.float32)
                moved = jnp.dot(s_ref[s, here, :], shift, preferred_element_type=jnp.float32)
                one = jnp.where(lanes == 0, column(cols, 11 + 2 * s), moved[:, :width])
                two = jnp.where(lanes == 0, column(cols, 10 + 2 * s), moved[:, width:])
                two = jnp.where(lanes == 1, column(cols, 11 + 2 * s), two)
                made.append(
                    column(cols, 3 * s) * x
                    + column(cols, 3 * s + 1) * one
                    + column(cols, 3 * s + 2) * two
                )
            g = (made[1] * made[2]).astype(jnp.bfloat16)
            f0_buf[here, :] = made[0]
            mix_buf[here, :] = made[0] * (column(cols, 9) * g.astype(jnp.float32))
            if per == 1:
                gated[block, r : r + sub, :] = g
            else:
                parts.append(g.astype(jnp.float32))
        for q in range(per):
            peer = block * per + q
            if per > 1:
                begin = q * group % sub
                piece = parts[q * group // sub][begin : begin + group]
                gated[peer] = piece.astype(jnp.bfloat16)
            o = lax.rem(peer - me + n, n)

            @pl.when(o > 0)
            def _():
                send_x(o).start()

        return carry

    lax.fori_loop(1, steps + 1, feature, 0)
    own_x = pltpu.make_async_copy(gated.at[me], x_in.at[me], own_sem.at[1])
    own_x.start()
    own_h.wait()
    loads[3].wait()
    loads[4].wait()

    def wait_all(make):
        def body(o, carry):
            make(o).wait()
            return carry

        lax.fori_loop(1, n, body, 0)

    wait_all(send_h)

    def filter_rows(r, carry):
        begin = pl.multiple_of(r * rows, rows)

        def load(a):
            return h_in[a, pl.ds(begin, rows), :]

        filt_buf[r] = forward(load, twist, mats, spec_buf, n, rows, width)
        return carry

    lax.fori_loop(0, group // rows, filter_rows, 0)
    own_x.wait()
    wait_all(send_x)

    def send_y(c, o):
        span = pl.ds(c * part, part)
        return sent(y_out, y_in, y_send.at[c, o], y_recv.at[c, o], o, span)

    def conv_rows(r, carry):
        begin = pl.multiple_of(r * rows, rows)

        def load(a):
            return x_in[a, pl.ds(begin, rows), :]

        def store(a, value):
            y_out[a, pl.ds(begin, rows), :] = value

        fx = forward(load, twist, mats, spec_buf, n, rows, width)
        xr, xi = fx[:, :width], fx[:, width:]
        hr, hi = filt_buf[r, :, :width], filt_buf[r, :, width:]
        prod = jnp.concatenate([xr * hr - xi * hi, xr * hi + xi * hr], axis=1)
        backward(prod, store, twist, mats, spec_buf, n, rows, width)
        return carry

    own_y = []
    per_chunk = part // rows
    for c in range(chunks):
        lax.fori_loop(c * per_chunk, (c + 1) * per_chunk, conv_rows, 0)
        start_all(functools.partial(send_y, c), 1, n)
        span = pl.ds(c * part, part)
        own_y.append(
            pltpu.make_async_copy(y_out.at[me, span], y_in.at[me, span], own_sem.at[2 + c])
        )
        own_y[c].start()

    sum_out[...] = jnp.zeros_like(sum_out)
    for c in range(chunks):

        def mix(source):
            begin = pl.multiple_of(source * group + c * part, part)
            y = y_in[source, pl.ds(c * part, part), :].astype(jnp.float32)
            mixed = f0_buf[pl.ds(begin, part), :] * y + mix_buf[pl.ds(begin, part), :]
            mix_buf[pl.ds(begin, part), :] = mixed
            sum_out[...] += jnp.sum((mixed * mixed).reshape(part // 8, 8, width), axis=0)

        own_y[c].wait()
        mix(me)

        def finish(o, carry):
            send_y(c, o).wait()
            mix(lax.rem(me - o + n, n))
            return carry

        lax.fori_loop(1, n, finish, 0)

    shared = []
    for o in range(1, cores):
        shared.append(
            pltpu.make_async_remote_copy(
                src_ref=sum_out, dst_ref=sum_in.at[core],
                send_sem=sum_send.at[o], recv_sem=sum_recv.at[o],
                device_id={"chan": lax.rem(core + o, cores)}, device_id_type=mesh_id,
            )
        )
        shared[-1].start()
    total = sum_out[...]
    for o in range(1, cores):
        shared[o - 1].wait()
        total = total + sum_in[lax.rem(core - o + cores, cores)]
    total = jnp.sum(total, axis=0, keepdims=True)
    inv_rms = lax.rsqrt(total / C + EPS)

    def normalize(b, carry):
        begin = pl.multiple_of(b * tall, tall)
        out_ref[pl.ds(begin, tall), :] = (mix_buf[pl.ds(begin, tall), :] * inv_rms).astype(
            jnp.bfloat16
        )
        return carry

    lax.fori_loop(0, steps, normalize, 0)


def halves_kernel(
    early, s_hbm, w_hbm, g_hbm, h_hbm, twist_hbm, mats_hbm, out_ref,
    s_ref, w_ref, g_ref, twist, mats, halo_out, halo_in, cols_buf, gated, f0_buf, mix_buf, h_in, x_in, y_out, y_in,
    sum_out, sum_in, spec_buf, filt_buf, filt_half,
    halo_sem, h_send, h_low, h_high, x_send, x_low, x_high, x_part, y_send, y_part, y_late, sum_send, sum_recv, own_sem,
    load_sem,
):
    n, cores = lax.axis_size("seq"), sum_in.shape[0]
    chans, width = gated.shape
    half = n // 2
    pair = chans // half
    late = pair - early
    rows = spec_buf.shape[1]
    me = lax.axis_index("seq")
    core = lax.axis_index("chan")
    mesh_id = pl.DeviceIdType.MESH
    low = me < half
    high = jnp.logical_not(low)
    base = lax.rem(me, half)
    slot = me * pair

    loads = [
        pltpu.make_async_copy(src, dst, load_sem.at[i])
        for i, (src, dst) in enumerate(
            [(s_hbm, s_ref), (w_hbm, w_ref), (g_hbm, g_ref), (twist_hbm, twist), (mats_hbm, mats)]
        )
    ]
    for copy in loads:
        copy.start()

    barrier = pltpu.get_barrier_semaphore()

    def greet(o, carry):
        peer = lax.rem(me + o, n)
        pl.semaphore_signal(barrier, inc=1, device_id={"seq": peer}, device_id_type=mesh_id)
        return carry

    lax.fori_loop(1, n, greet, 0)
    for o in range(1, cores):
        pl.semaphore_signal(
            barrier, inc=1, device_id={"chan": lax.rem(core + o, cores)}, device_id_type=mesh_id
        )

    def span(start, count):
        return pl.ds(pl.multiple_of(start, 16), count)

    def send(src, at, dst, to, count, sent, got, peer):
        pltpu.make_async_remote_copy(
            src_ref=src.at[span(at, count)], dst_ref=dst.at[span(to, count)], send_sem=sent, recv_sem=got,
            device_id={"seq": peer}, device_id_type=mesh_id,
        ).start()

    def keep(src, at, dst, to, count, sem):
        copy = pltpu.make_async_copy(src.at[span(at, count)], dst.at[span(to, count)], sem)
        copy.start()

    def drain(sem, count):
        pltpu.make_async_copy(x_in.at[pl.ds(0, count)], x_in.at[pl.ds(0, count)], sem).wait()

    def around(first, body):
        def step(o, carry):
            body(lax.rem(base + o, half))
            return carry

        lax.fori_loop(first, half, step, 0)

    pl.semaphore_wait(barrier, n - 1 + cores - 1)

    @pl.when(low)
    def _():
        around(0, lambda b: send(h_hbm, b * pair + early, h_in, slot, late, h_send, h_low, half + b))

    @pl.when(high)
    def _():
        around(0, lambda a: send(h_hbm, a * pair, h_in, slot, early, h_send, h_high, a))

    row = lax.broadcasted_iota(jnp.int32, (16, width), 0)
    lane = lax.broadcasted_iota(jnp.int32, (16, width), 1)
    last = None
    loads[0].wait()
    for s in range(3):
        pick = ((row == 10 + 2 * s) & (lane == width - 2)) | (
            (row == 11 + 2 * s) & (lane == width - 1)
        )
        got = lax.dot_general(
            jnp.where(pick, 1.0, 0.0).astype(jnp.bfloat16),
            s_ref[s],
            (((1,), (1,)), ((), ())),
            preferred_element_type=jnp.float32,
        )
        last = got if last is None else last + got
    halo_out[...] = last.astype(jnp.bfloat16)

    halo = pltpu.make_async_remote_copy(
        src_ref=halo_out, dst_ref=halo_in, send_sem=halo_sem.at[0], recv_sem=halo_sem.at[1],
        device_id={"seq": lax.rem(me + 1, n)}, device_id_type=mesh_id,
    )
    halo.start()

    @pl.when(low)
    def _():
        around(1, lambda a: send(h_hbm, a * pair, h_in, slot, pair, h_send, h_low, a))
        keep(h_hbm, base * pair, h_in, slot, pair, own_sem.at[0])

    @pl.when(high)
    def _():
        around(1, lambda b: send(h_hbm, b * pair + early, h_in, slot, late, h_send, h_high, half + b))
        keep(h_hbm, base * pair + early, h_in, slot, late, own_sem.at[0])

    loads[1].wait()
    loads[2].wait()
    halo.wait()
    for s in range(3):
        cols_buf[3 * s : 3 * s + 3, :] = w_ref[s]
    cols_buf[9:10, :] = g_ref[...]
    cols_buf[10:16, :] = jnp.where(me > 0, halo_in[...].astype(jnp.float32)[10:16], 0.0)

    lanes = lax.broadcasted_iota(jnp.int32, (pair, width), 1)
    source = lax.broadcasted_iota(jnp.int32, (width, 2 * width), 0)
    target = lax.broadcasted_iota(jnp.int32, (width, 2 * width), 1)
    moves = (target == source + 1) & (target < width)
    moves = moves | (target == source + width + 2)
    shift = jnp.where(moves, 1.0, 0.0).astype(jnp.bfloat16)

    def feature(step, carry):
        group = lax.rem(base + step, half)
        begin = pl.multiple_of(group * pair, pair)
        cols = cols_buf[:, pl.ds(begin, pair)].T
        here = pl.ds(begin, pair)
        made = []
        for s in range(3):
            x = s_ref[s, here, :].astype(jnp.float32)
            moved = jnp.dot(s_ref[s, here, :], shift, preferred_element_type=jnp.float32)
            one = jnp.where(lanes == 0, column(cols, 11 + 2 * s), moved[:, :width])
            two = jnp.where(lanes == 0, column(cols, 10 + 2 * s), moved[:, width:])
            two = jnp.where(lanes == 1, column(cols, 11 + 2 * s), two)
            made.append(
                column(cols, 3 * s) * x
                + column(cols, 3 * s + 1) * one
                + column(cols, 3 * s + 2) * two
            )
        g = (made[1] * made[2]).astype(jnp.bfloat16)
        f0_buf[here, :] = made[0]
        mix_buf[here, :] = made[0] * (column(cols, 9) * g.astype(jnp.float32))
        gated[here, :] = g

        @pl.when(low)
        def _():
            send(gated, begin + early, x_in, slot, late, x_send, x_low, half + group)

            @pl.when(group != base)
            def _():
                send(gated, begin, x_in, slot, pair, x_send, x_low, group)

        @pl.when(high & (group != base))
        def _():
            send(gated, begin + early, x_in, slot, late, x_send, x_high, half + group)

        return carry

    lax.fori_loop(0, half, feature, 0)
    parts = early // rows

    @pl.when(low)
    def _():
        keep(gated, base * pair, x_in, slot, pair, own_sem.at[1])

    @pl.when(high)
    def _():
        def part(k, carry):
            around(0, lambda a: send(
                gated, a * pair + k * rows, x_in, slot + k * rows, rows, x_send, x_part.at[k], a
            ))
            return carry

        lax.fori_loop(0, parts, part, 0)
        keep(gated, base * pair + early, x_in, slot, late, own_sem.at[1])

    loads[3].wait()
    loads[4].wait()

    def forward_rows(buf, first, blocks):
        def load(a):
            return buf[span(a * pair + first, rows), :]

        return forward(load, twist, mats, spec_buf, blocks, rows, width)

    def convolve(first, filt, blocks):
        def store(a, value):
            y_out[span(a * pair + first, rows), :] = value

        fx = forward_rows(x_in, first, blocks)
        xr, xi = fx[:, :width], fx[:, width:]
        hr, hi = filt[:, :width], filt[:, width:]
        prod = jnp.concatenate([xr * hr - xi * hi, xr * hi + xi * hr], axis=1)
        backward(prod, store, twist, mats, spec_buf, blocks, rows, width)

    @pl.when(low)
    def _():
        drain(h_low, (half - 1) * pair)
        drain(own_sem.at[0], pair)
        drain(x_low, (half - 1) * pair)
        drain(own_sem.at[1], pair)

        def late_rows(r, carry):
            first = early + r * rows
            filt_half[...] = 2.0 * forward_rows(h_in, first, half)
            convolve(first, filt_half, half)
            return carry

        lax.fori_loop(0, late // rows, late_rows, 0)
        around(1, lambda a: send(
            y_out, a * pair + early, y_in, base * pair + early, late, y_send, y_late, a
        ))
        keep(y_out, slot + early, y_in, base * pair + early, late, own_sem.at[2])
        drain(h_high, half * early)

    @pl.when(high)
    def _():
        drain(h_low, half * late)
        drain(h_high, (half - 1) * late)
        drain(own_sem.at[0], late)

    blocks_here = jnp.where(low, early // rows, late // rows)

    def filter_rows(r, carry):
        filt_buf[r] = forward_rows(h_in, r * rows, n)
        return carry

    lax.fori_loop(0, blocks_here, filter_rows, 0)

    @pl.when(high)
    def _():
        drain(x_low, half * late)
        drain(x_high, (half - 1) * late)
        drain(own_sem.at[1], late)

    def conv_rows(r, carry):
        first = r * rows

        @pl.when(low)
        def _():
            drain(x_part.at[r], half * rows)

        convolve(first, filt_buf.at[r], n)

        @pl.when(low)
        def _():
            to = base * pair + first
            around(0, lambda b: send(
                y_out, (half + b) * pair + first, y_in, to, rows, y_send, y_part.at[r], half + b
            ))
            around(1, lambda a: send(y_out, a * pair + first, y_in, to, rows, y_send, y_part.at[r], a))
            keep(y_out, slot + first, y_in, to, rows, own_sem.at[3])

        @pl.when(high)
        def _():
            to = base * pair + early + first
            around(1, lambda b: send(
                y_out, (half + b) * pair + first, y_in, to, rows, y_send, y_late, half + b
            ))
            keep(y_out, slot + first, y_in, to, rows, own_sem.at[2])

        return carry

    lax.fori_loop(0, blocks_here, conv_rows, 0)

    sum_out[...] = jnp.zeros_like(sum_out)

    def mix(begin, count):
        here = span(begin, count)
        mixed = f0_buf[here, :] * y_in[here, :].astype(jnp.float32) + mix_buf[here, :]
        mix_buf[here, :] = mixed
        sum_out[...] += jnp.sum((mixed * mixed).reshape(count // 8, 8, width), axis=0)

    drain(own_sem.at[2], late)
    drain(y_late, (half - 1) * late)
    around(0, lambda a: mix(a * pair + early, late))

    @pl.when(low)
    def _():
        drain(own_sem.at[3], early)

    def finish(k, carry):
        @pl.when(low)
        def _():
            drain(y_part.at[k], (half - 1) * rows)

        @pl.when(high)
        def _():
            drain(y_part.at[k], half * rows)

        around(0, lambda a: mix(a * pair + k * rows, rows))
        return carry

    lax.fori_loop(0, parts, finish, 0)

    shared = []
    for o in range(1, cores):
        shared.append(
            pltpu.make_async_remote_copy(
                src_ref=sum_out, dst_ref=sum_in.at[core],
                send_sem=sum_send.at[o], recv_sem=sum_recv.at[o],
                device_id={"chan": lax.rem(core + o, cores)}, device_id_type=mesh_id,
            )
        )
        shared[-1].start()
    total = sum_out[...]
    for o in range(1, cores):
        shared[o - 1].wait()
        total = total + sum_in[lax.rem(core - o + cores, cores)]
    total = jnp.sum(total, axis=0, keepdims=True)
    inv_rms = lax.rsqrt(total / C + EPS)

    def normalize(b, carry):
        begin = pl.multiple_of(b * pair, pair)
        out_ref[pl.ds(begin, pair), :] = (mix_buf[pl.ds(begin, pair), :] * inv_rms).astype(
            jnp.bfloat16
        )
        return carry

    lax.fori_loop(0, half, normalize, 0)

    @pl.when(low)
    def _():
        drain(h_send, (half - 1) * pair + half * late)
        drain(x_send, (half - 1) * pair + half * late)
        drain(y_send, (n - 1) * early + (half - 1) * late)

    @pl.when(high)
    def _():
        drain(h_send, half * early + (half - 1) * late)
        drain(x_send, half * early + (half - 1) * late)
        drain(y_send, (half - 1) * late)


CHUNKS = 2
ROWS = 32


def halves(streams, feat_weights, skip_gain, filter_taps, early):
    n, cores = lax.axis_size("seq"), lax.axis_size("chan")
    chans, width = filter_taps.shape
    pair = 2 * chans // n
    late = pair - early
    twist, mats = tables(n, width)
    dma = pltpu.SemaphoreType.DMA
    one = dma(())
    half = pltpu.VMEM((n * pair, width), jnp.bfloat16)
    whole = pltpu.VMEM((chans, width), jnp.float32)
    parts = early // ROWS
    most = max(early, late) // ROWS
    return pl.pallas_call(
        functools.partial(halves_kernel, early),
        in_specs=[pl.BlockSpec(memory_space=pl.ANY)] * 6,
        out_specs=pl.BlockSpec(memory_space=pltpu.VMEM),
        out_shape=jax.ShapeDtypeStruct((chans, width), jnp.bfloat16),
        scratch_shapes=[
            pltpu.VMEM(streams.shape, jnp.bfloat16),
            pltpu.VMEM((3, TAPS, chans), jnp.float32),
            pltpu.VMEM((1, chans), jnp.float32),
            pltpu.VMEM(twist.shape, jnp.float32),
            pltpu.VMEM(mats.shape, jnp.bfloat16),
            pltpu.VMEM((16, chans), jnp.bfloat16),
            pltpu.VMEM((16, chans), jnp.bfloat16),
            pltpu.VMEM((16, chans), jnp.float32),
            pltpu.VMEM((chans, width), jnp.bfloat16), whole, whole, half, half, half,
            pltpu.VMEM((chans, width), jnp.bfloat16),
            pltpu.VMEM((8, width), jnp.float32),
            pltpu.VMEM((cores, 8, width), jnp.float32),
            pltpu.VMEM((n + 1, ROWS, 2 * width), jnp.float32),
            pltpu.VMEM((most, (n + 1) * ROWS, 2 * width), jnp.float32),
            pltpu.VMEM(((n // 2 + 1) * ROWS, 2 * width), jnp.float32),
            dma((2,)),
            one, one, one, one, one, one, dma((parts,)), one, dma((parts,)), one,
            dma((cores,)), dma((cores,)), dma((4,)), dma((5,)),
        ],
        compiler_params=pltpu.CompilerParams(
            collective_id=0, has_side_effects=True, vmem_limit_bytes=60 << 20
        ),
    )(
        streams, feat_weights.transpose(0, 2, 1), skip_gain[None, :],
        filter_taps, jnp.asarray(twist), jnp.asarray(mats),
    )


def local(streams, feat_weights, skip_gain, filter_taps):
    n, cores = lax.axis_size("seq"), lax.axis_size("chan")
    chans, width = filter_taps.shape
    group = chans // n
    if n % 2 == 0 and chans % n == 0 and 2 * group % 128 == 0:
        early = 2 * group * 5 // 8 // ROWS * ROWS
        return halves(streams, feat_weights, skip_gain, filter_taps, early)
    chunks = CHUNKS if group % (16 * CHUNKS) == 0 else 1
    rows = math.gcd(group // chunks, 32)
    twist, mats = tables(n, width)
    vmem = pl.BlockSpec(memory_space=pltpu.VMEM)
    dma = pltpu.SemaphoreType.DMA
    half = pltpu.VMEM((n, group, width), jnp.bfloat16)
    whole = pltpu.VMEM((chans, width), jnp.float32)
    return pl.pallas_call(
        functools.partial(fused_kernel, chunks),
        in_specs=[pl.BlockSpec(memory_space=pl.ANY)] * 6,
        out_specs=vmem,
        out_shape=jax.ShapeDtypeStruct((chans, width), jnp.bfloat16),
        scratch_shapes=[
            pltpu.VMEM(streams.shape, jnp.bfloat16),
            pltpu.VMEM((3, TAPS, chans), jnp.float32),
            pltpu.VMEM((1, chans), jnp.float32),
            pltpu.VMEM(twist.shape, jnp.float32),
            pltpu.VMEM(mats.shape, jnp.bfloat16),
            pltpu.VMEM((16, chans), jnp.bfloat16),
            pltpu.VMEM((16, chans), jnp.bfloat16),
            pltpu.VMEM((16, chans), jnp.float32),
            half, whole, whole, half, half, half, half,
            pltpu.VMEM((8, width), jnp.float32),
            pltpu.VMEM((cores, 8, width), jnp.float32),
            pltpu.VMEM((n + 1, rows, 2 * width), jnp.float32),
            pltpu.VMEM((group // rows, (n + 1) * rows, 2 * width), jnp.float32),
            dma((2,)),
            dma((n,)), dma((n,)), dma((n,)), dma((n,)),
            dma((chunks, n)), dma((chunks, n)),
            dma((cores,)), dma((cores,)), dma((2 + chunks,)), dma((5,)),
        ],
        compiler_params=pltpu.CompilerParams(
            collective_id=0, has_side_effects=True, vmem_limit_bytes=60 << 20
        ),
    )(
        streams, feat_weights.transpose(0, 2, 1), skip_gain[None, :],
        filter_taps.reshape(n, group, width), jnp.asarray(twist), jnp.asarray(mats),
    )


def solution(mesh):
    placed = (P(None, "chan", "seq"), P(None, "chan", None), P("chan"), P("chan", "seq"))
    return jax.shard_map(
        local, mesh=mesh, in_specs=placed, out_specs=P("chan", "seq"), check_vma=False
    )
```

```python
import functools
import math

import jax
import jax.numpy as jnp
import numpy as np
from jax import lax
from jax.experimental import pallas as pl
from jax.experimental.pallas import tpu as pltpu
from jax.sharding import PartitionSpec as P

C = 4096
TAPS = 3
EPS = 1e-05


def add(a, b):
    if a is None:
        return b
    return a if b is None else a + b


def sub(a, b):
    if b is None:
        return a
    return -b if a is None else a - b


def times(pair, angle):
    re, im = pair
    c, s = math.cos(angle), math.sin(angle)
    if abs(s) < 1e-12 and c > 0:
        return pair
    if abs(c) < 1e-12:
        turned = (None if im is None else -im, re)
        return turned if s > 0 else (None if turned[0] is None else -turned[0], -re)
    if im is None:
        return (re * c, re * s)
    return (re * c - im * s, re * s + im * c)


def real_fft(xs, n):
    if n == 2:
        return [(xs[0], None), (xs[0], None)]
    even = real_fft(xs[0::2], n // 2)
    odd = real_fft(xs[1::2], n // 2)
    out = [None] * (n // 2 + 1)
    for k in range(n // 4 + 1):
        er, ei = even[k]
        tr, ti = times(odd[k], -2.0 * math.pi * k / n)
        out[k] = (add(er, tr), add(ei, ti))
        if n // 2 - k != k:
            out[n // 2 - k] = (sub(er, tr), sub(ti, ei))
    return out


def real_ifft(spec, n):
    if n == 2:
        return [spec[0][0] + spec[1][0]]
    even, odd = [], []
    for k in range(n // 4 + 1):
        ar, ai = spec[k]
        br, bi = spec[n // 2 - k]
        if n // 2 - k == k:
            er, ei, dr, di = ar + ar, None, None, add(ai, ai)
            even.append((er, ei))
            odd.append((-di if di is not None else None, None))
            continue
        even.append((ar + br, sub(ai, bi)))
        odd.append(times((ar - br, add(ai, bi)), 2.0 * math.pi * k / n))
    first = real_ifft(even, n // 2)
    second = real_ifft(odd, n // 2)
    out = []
    for a, b in zip(first, second):
        out += [a, b]
    return out


def tables(blocks, width):
    total = 2 * blocks * width
    k1 = np.arange(blocks + 1)[:, None]
    i = np.arange(width)[None, :]
    ang = 2.0 * np.pi * ((k1 * i) % total) / total
    twist = np.stack([np.cos(ang), np.sin(ang)]).astype(np.float32)[:, :, None, :]
    j = np.arange(width)
    ang = 2.0 * np.pi * ((j[:, None] * j[None, :]) % width) / width
    c, s = np.cos(ang), np.sin(ang)
    forward = np.block([[c, -s], [s, c]])
    inverse = np.block([[c, s], [-s, c]]) / total
    out = []
    for m in (forward, inverse):
        hi = m.astype(np.float32).astype(jnp.bfloat16)
        lo = (m - hi.astype(np.float64)).astype(np.float32).astype(jnp.bfloat16)
        out += [hi, lo]
    return twist, np.stack(out)


def split_dot(x, hi_w, lo_w):
    hi = x.astype(jnp.bfloat16)
    lo = (x - hi.astype(jnp.float32)).astype(jnp.bfloat16)
    dot = functools.partial(jnp.dot, preferred_element_type=jnp.float32)
    return dot(hi, hi_w) + (dot(lo, hi_w) + dot(hi, lo_w))


def forward(load, twist, mats, buf, blocks, rows, width):
    xs = [load(a).astype(jnp.float32) for a in range(blocks)]
    for k, (re, im) in enumerate(real_fft(xs, 2 * blocks)):
        tc, ts = twist[0, k], twist[1, k]
        if k == 0:
            new_re, new_im = re, jnp.zeros_like(re)
        elif im is None:
            new_re, new_im = re * tc, -(re * ts)
        else:
            new_re, new_im = re * tc + im * ts, im * tc - re * ts
        buf[k, :, :width] = new_re
        buf[k, :, width:] = new_im
    flat = (blocks + 1) * rows
    return split_dot(buf[...].reshape(flat, 2 * width), mats[0], mats[1])


def backward(prod, store, twist, mats, buf, blocks, rows, width):
    back = split_dot(prod, mats[2], mats[3])
    buf[...] = back.reshape(blocks + 1, rows, 2 * width)
    spec = []
    for k in range(blocks + 1):
        re, im = buf[k, :, :width], buf[k, :, width:]
        tc, ts = twist[0, k], twist[1, k]
        out_re = re if k == 0 else re * tc - im * ts
        out_im = None if k in (0, blocks) else re * ts + im * tc
        spec.append((out_re, out_im))
    for a, y in enumerate(real_ifft(spec, 2 * blocks)):
        store(a, y.astype(jnp.bfloat16))


def column(cols, j):
    return cols[:, j : j + 1]


def fused_kernel(
    chunks, s_hbm, w_hbm, g_hbm, h_ref, twist_hbm, mats_hbm, out_ref, inv_ref,
    s_ref, w_ref, g_ref, twist, mats, halo_out, halo_in, cols_buf, gated, f0_buf, mix_buf, h_in, x_in, y_out, y_in,
    sum_out, sum_in, spec_buf, filt_buf,
    halo_sem, h_send, h_recv, x_send, x_recv, y_send, y_recv, sum_send, sum_recv, own_sem,
    load_sem,
):
    n, group, width = gated.shape
    part = group // chunks
    rows = math.gcd(part, 32)
    chans = n * group
    cores = sum_in.shape[0]
    me = lax.axis_index("seq")
    core = lax.axis_index("chan")
    mesh_id = pl.DeviceIdType.MESH

    loads = [
        pltpu.make_async_copy(src, dst, load_sem.at[i])
        for i, (src, dst) in enumerate(
            [(s_hbm, s_ref), (w_hbm, w_ref), (g_hbm, g_ref), (twist_hbm, twist), (mats_hbm, mats)]
        )
    ]
    for copy in loads:
        copy.start()

    barrier = pltpu.get_barrier_semaphore()

    def greet(o, carry):
        peer = lax.rem(me + o, n)
        pl.semaphore_signal(barrier, inc=1, device_id={"seq": peer}, device_id_type=mesh_id)
        return carry

    lax.fori_loop(1, n, greet, 0)
    for o in range(1, cores):
        pl.semaphore_signal(
            barrier, inc=1, device_id={"chan": lax.rem(core + o, cores)}, device_id_type=mesh_id
        )

    def sent(src, dst, send, recv, o, span):
        peer = lax.rem(me + o, n)
        return pltpu.make_async_remote_copy(
            src_ref=src.at[peer, span], dst_ref=dst.at[me, span],
            send_sem=send, recv_sem=recv,
            device_id={"seq": peer}, device_id_type=mesh_id,
        )

    everything = pl.ds(0, group)

    def send_h(o):
        return sent(h_ref, h_in, h_send.at[o], h_recv.at[o], o, everything)

    def send_x(o):
        return sent(gated, x_in, x_send.at[o], x_recv.at[o], o, everything)

    def start_all(make, first, end):
        def body(o, carry):
            make(o).start()
            return carry

        lax.fori_loop(first, end, body, 0)

    row = lax.broadcasted_iota(jnp.int32, (16, width), 0)
    lane = lax.broadcasted_iota(jnp.int32, (16, width), 1)
    last = None
    pl.semaphore_wait(barrier, n - 1 + cores - 1)
    start_all(send_h, 1, 1 + n // 2)
    loads[0].wait()
    for s in range(3):
        pick = ((row == 10 + 2 * s) & (lane == width - 2)) | (
            (row == 11 + 2 * s) & (lane == width - 1)
        )
        got = lax.dot_general(
            jnp.where(pick, 1.0, 0.0).astype(jnp.bfloat16),
            s_ref[s],
            (((1,), (1,)), ((), ())),
            preferred_element_type=jnp.float32,
        )
        last = got if last is None else last + got
    halo_out[...] = last.astype(jnp.bfloat16)

    halo = pltpu.make_async_remote_copy(
        src_ref=halo_out, dst_ref=halo_in, send_sem=halo_sem.at[0], recv_sem=halo_sem.at[1],
        device_id={"seq": lax.rem(me + 1, n)}, device_id_type=mesh_id,
    )
    halo.start()

    start_all(send_h, 1 + n // 2, n)
    own_h = pltpu.make_async_copy(h_ref.at[me], h_in.at[me], own_sem.at[0])
    own_h.start()
    loads[1].wait()
    loads[2].wait()
    halo.wait()
    for s in range(3):
        cols_buf[3 * s : 3 * s + 3, :] = w_ref[s]
    cols_buf[9:10, :] = g_ref[...]
    cols_buf[10:16, :] = jnp.where(me > 0, halo_in[...].astype(jnp.float32)[10:16], 0.0)

    tall = math.gcd(chans, 256)
    per = tall // group if tall > group else 1
    steps = chans // tall
    sub = tall
    lanes = lax.broadcasted_iota(jnp.int32, (sub, width), 1)

    source = lax.broadcasted_iota(jnp.int32, (width, 2 * width), 0)
    target = lax.broadcasted_iota(jnp.int32, (width, 2 * width), 1)
    moves = (target == source + 1) & (target < width)
    moves = moves | (target == source + width + 2)
    shift = jnp.where(moves, 1.0, 0.0).astype(jnp.bfloat16)

    def feature(step, carry):
        block = lax.rem(me // per + step, steps)
        begin = pl.multiple_of(block * tall, tall)
        columns = cols_buf[:, pl.ds(begin, tall)].T
        parts = []
        for r in range(0, tall, sub):
            cols = columns[r : r + sub]
            here = pl.ds(begin + r, sub)
            made = []
            for s in range(3):
                x = s_ref[s, here, :].astype(jnp.float32)
                moved = jnp.dot(s_ref[s, here, :], shift, preferred_element_type=jnp.float32)
                one = jnp.where(lanes == 0, column(cols, 11 + 2 * s), moved[:, :width])
                two = jnp.where(lanes == 0, column(cols, 10 + 2 * s), moved[:, width:])
                two = jnp.where(lanes == 1, column(cols, 11 + 2 * s), two)
                made.append(
                    column(cols, 3 * s) * x
                    + column(cols, 3 * s + 1) * one
                    + column(cols, 3 * s + 2) * two
                )
            g = (made[1] * made[2]).astype(jnp.bfloat16)
            f0_buf[here, :] = made[0]
            mix_buf[here, :] = made[0] * (column(cols, 9) * g.astype(jnp.float32))
            if per == 1:
                gated[block, r : r + sub, :] = g
            else:
                parts.append(g.astype(jnp.float32))
        for q in range(per):
            peer = block * per + q
            if per > 1:
                begin = q * group % sub
                piece = parts[q * group // sub][begin : begin + group]
                gated[peer] = piece.astype(jnp.bfloat16)
            o = lax.rem(peer - me + n, n)

            @pl.when(o > 0)
            def _():
                send_x(o).start()

        return carry

    lax.fori_loop(1, steps + 1, feature, 0)
    own_x = pltpu.make_async_copy(gated.at[me], x_in.at[me], own_sem.at[1])
    own_x.start()
    own_h.wait()
    loads[3].wait()
    loads[4].wait()

    def wait_all(make):
        def body(o, carry):
            make(o).wait()
            return carry

        lax.fori_loop(1, n, body, 0)

    wait_all(send_h)

    def filter_rows(r, carry):
        begin = pl.multiple_of(r * rows, rows)

        def load(a):
            return h_in[a, pl.ds(begin, rows), :]

        filt_buf[r] = forward(load, twist, mats, spec_buf, n, rows, width)
        return carry

    lax.fori_loop(0, group // rows, filter_rows, 0)
    own_x.wait()
    wait_all(send_x)

    def send_y(c, o):
        span = pl.ds(c * part, part)
        return sent(y_out, y_in, y_send.at[c, o], y_recv.at[c, o], o, span)

    def conv_rows(r, carry):
        begin = pl.multiple_of(r * rows, rows)

        def load(a):
            return x_in[a, pl.ds(begin, rows), :]

        def store(a, value):
            y_out[a, pl.ds(begin, rows), :] = value

        fx = forward(load, twist, mats, spec_buf, n, rows, width)
        xr, xi = fx[:, :width], fx[:, width:]
        hr, hi = filt_buf[r, :, :width], filt_buf[r, :, width:]
        prod = jnp.concatenate([xr * hr - xi * hi, xr * hi + xi * hr], axis=1)
        backward(prod, store, twist, mats, spec_buf, n, rows, width)
        return carry

    own_y = []
    per_chunk = part // rows
    for c in range(chunks):
        lax.fori_loop(c * per_chunk, (c + 1) * per_chunk, conv_rows, 0)
        start_all(functools.partial(send_y, c), 1, n)
        span = pl.ds(c * part, part)
        own_y.append(
            pltpu.make_async_copy(y_out.at[me, span], y_in.at[me, span], own_sem.at[2 + c])
        )
        own_y[c].start()

    sum_out[...] = jnp.zeros_like(sum_out)
    for c in range(chunks):

        def mix(source):
            begin = pl.multiple_of(source * group + c * part, part)
            y = y_in[source, pl.ds(c * part, part), :].astype(jnp.float32)
            mixed = f0_buf[pl.ds(begin, part), :] * y + mix_buf[pl.ds(begin, part), :]
            out_ref[pl.ds(begin, part), :] = mixed.astype(jnp.float32)
            sum_out[...] += jnp.sum((mixed * mixed).reshape(part // 8, 8, width), axis=0)

        own_y[c].wait()
        mix(me)

        def finish(o, carry):
            send_y(c, o).wait()
            mix(lax.rem(me - o + n, n))
            return carry

        lax.fori_loop(1, n, finish, 0)

    shared = []
    for o in range(1, cores):
        shared.append(
            pltpu.make_async_remote_copy(
                src_ref=sum_out, dst_ref=sum_in.at[core],
                send_sem=sum_send.at[o], recv_sem=sum_recv.at[o],
                device_id={"chan": lax.rem(core + o, cores)}, device_id_type=mesh_id,
            )
        )
        shared[-1].start()
    total = sum_out[...]
    for o in range(1, cores):
        shared[o - 1].wait()
        total = total + sum_in[lax.rem(core - o + cores, cores)]
    total = jnp.sum(total, axis=0, keepdims=True)
    inv_rms = lax.rsqrt(total / C + EPS)

    inv_ref[...] = inv_rms


CHUNKS = 2


def local(streams, feat_weights, skip_gain, filter_taps):
    n, cores = lax.axis_size("seq"), lax.axis_size("chan")
    chans, width = filter_taps.shape
    group = chans // n
    chunks = CHUNKS if group % (16 * CHUNKS) == 0 else 1
    rows = math.gcd(group // chunks, 32)
    twist, mats = tables(n, width)
    vmem = pl.BlockSpec(memory_space=pltpu.VMEM)
    dma = pltpu.SemaphoreType.DMA
    half = pltpu.VMEM((n, group, width), jnp.bfloat16)
    whole = pltpu.VMEM((chans, width), jnp.float32)
    mixed, inv = pl.pallas_call(
        functools.partial(fused_kernel, chunks),
        in_specs=[pl.BlockSpec(memory_space=pl.ANY)] * 6,
        out_specs=[vmem, vmem],
        out_shape=[pltpu.VMEM((chans, width), jnp.float32), pltpu.VMEM((1, width), jnp.float32)],
        scratch_shapes=[
            pltpu.VMEM(streams.shape, jnp.bfloat16),
            pltpu.VMEM((3, TAPS, chans), jnp.float32),
            pltpu.VMEM((1, chans), jnp.float32),
            pltpu.VMEM(twist.shape, jnp.float32),
            pltpu.VMEM(mats.shape, jnp.bfloat16),
            pltpu.VMEM((16, chans), jnp.bfloat16),
            pltpu.VMEM((16, chans), jnp.bfloat16),
            pltpu.VMEM((16, chans), jnp.float32),
            half, whole, whole, half, half, half, half,
            pltpu.VMEM((8, width), jnp.float32),
            pltpu.VMEM((cores, 8, width), jnp.float32),
            pltpu.VMEM((n + 1, rows, 2 * width), jnp.float32),
            pltpu.VMEM((group // rows, (n + 1) * rows, 2 * width), jnp.float32),
            dma((2,)),
            dma((n,)), dma((n,)), dma((n,)), dma((n,)),
            dma((chunks, n)), dma((chunks, n)),
            dma((cores,)), dma((cores,)), dma((2 + chunks,)), dma((5,)),
        ],
        compiler_params=pltpu.CompilerParams(
            collective_id=0, has_side_effects=True, vmem_limit_bytes=60 << 20
        ),
    )(
        streams, feat_weights.transpose(0, 2, 1), skip_gain[None, :],
        filter_taps.reshape(n, group, width), jnp.asarray(twist), jnp.asarray(mats),
    )
    return (mixed.astype(jnp.float32) * inv).astype(jnp.bfloat16)


def solution(mesh):
    placed = (P(None, "chan", "seq"), P(None, "chan", None), P("chan"), P("chan", "seq"))
    return jax.shard_map(
        local, mesh=mesh, in_specs=placed, out_specs=P("chan", "seq"), check_vma=False
    )
```

```python
import functools
import math

import jax
import jax.numpy as jnp
import numpy as np
from jax import lax
from jax.experimental import pallas as pl
from jax.experimental.pallas import tpu as pltpu
from jax.sharding import PartitionSpec as P

C = 4096
TAPS = 3
EPS = 1e-05


def add(a, b):
    if a is None:
        return b
    return a if b is None else a + b


def sub(a, b):
    if b is None:
        return a
    return -b if a is None else a - b


def times(pair, angle):
    re, im = pair
    c, s = math.cos(angle), math.sin(angle)
    if abs(s) < 1e-12 and c > 0:
        return pair
    if abs(c) < 1e-12:
        turned = (None if im is None else -im, re)
        return turned if s > 0 else (None if turned[0] is None else -turned[0], -re)
    if im is None:
        return (re * c, re * s)
    return (re * c - im * s, re * s + im * c)


def real_fft(xs, n):
    if n == 2:
        return [(xs[0], None), (xs[0], None)]
    even = real_fft(xs[0::2], n // 2)
    odd = real_fft(xs[1::2], n // 2)
    out = [None] * (n // 2 + 1)
    for k in range(n // 4 + 1):
        er, ei = even[k]
        tr, ti = times(odd[k], -2.0 * math.pi * k / n)
        out[k] = (add(er, tr), add(ei, ti))
        if n // 2 - k != k:
            out[n // 2 - k] = (sub(er, tr), sub(ti, ei))
    return out


def real_ifft(spec, n):
    if n == 2:
        return [spec[0][0] + spec[1][0]]
    even, odd = [], []
    for k in range(n // 4 + 1):
        ar, ai = spec[k]
        br, bi = spec[n // 2 - k]
        if n // 2 - k == k:
            er, ei, dr, di = ar + ar, None, None, add(ai, ai)
            even.append((er, ei))
            odd.append((-di if di is not None else None, None))
            continue
        even.append((ar + br, sub(ai, bi)))
        odd.append(times((ar - br, add(ai, bi)), 2.0 * math.pi * k / n))
    first = real_ifft(even, n // 2)
    second = real_ifft(odd, n // 2)
    out = []
    for a, b in zip(first, second):
        out += [a, b]
    return out


def tables(blocks, width):
    total = 2 * blocks * width
    k1 = np.arange(blocks + 1)[:, None]
    i = np.arange(width)[None, :]
    ang = 2.0 * np.pi * ((k1 * i) % total) / total
    twist = np.stack([np.cos(ang), np.sin(ang)]).astype(np.float32)[:, :, None, :]
    j = np.arange(width)
    ang = 2.0 * np.pi * ((j[:, None] * j[None, :]) % width) / width
    c, s = np.cos(ang), np.sin(ang)
    forward = np.block([[c, -s], [s, c]])
    inverse = np.block([[c, s], [-s, c]]) / total
    out = []
    for m in (forward, inverse):
        hi = m.astype(np.float32).astype(jnp.bfloat16)
        lo = (m - hi.astype(np.float64)).astype(np.float32).astype(jnp.bfloat16)
        out += [hi, lo]
    return twist, np.stack(out)


def split_dot(x, hi_w, lo_w):
    hi = x.astype(jnp.bfloat16)
    lo = (x - hi.astype(jnp.float32)).astype(jnp.bfloat16)
    dot = functools.partial(jnp.dot, preferred_element_type=jnp.float32)
    return dot(hi, hi_w) + (dot(lo, hi_w) + dot(hi, lo_w))


def forward(load, twist, mats, buf, blocks, rows, width):
    xs = [load(a).astype(jnp.float32) for a in range(blocks)]
    for k, (re, im) in enumerate(real_fft(xs, 2 * blocks)):
        tc, ts = twist[0, k], twist[1, k]
        if k == 0:
            new_re, new_im = re, jnp.zeros_like(re)
        elif im is None:
            new_re, new_im = re * tc, -(re * ts)
        else:
            new_re, new_im = re * tc + im * ts, im * tc - re * ts
        buf[k, :, :width] = new_re
        buf[k, :, width:] = new_im
    flat = (blocks + 1) * rows
    return split_dot(buf[...].reshape(flat, 2 * width), mats[0], mats[1])


def backward(prod, store, twist, mats, buf, blocks, rows, width):
    back = split_dot(prod, mats[2], mats[3])
    buf[...] = back.reshape(blocks + 1, rows, 2 * width)
    spec = []
    for k in range(blocks + 1):
        re, im = buf[k, :, :width], buf[k, :, width:]
        tc, ts = twist[0, k], twist[1, k]
        out_re = re if k == 0 else re * tc - im * ts
        out_im = None if k in (0, blocks) else re * ts + im * tc
        spec.append((out_re, out_im))
    for a, y in enumerate(real_ifft(spec, 2 * blocks)):
        store(a, y.astype(jnp.bfloat16))


def column(cols, j):
    return cols[:, j : j + 1]


def fused_kernel(
    chunks, s_hbm, w_hbm, g_hbm, h_ref, twist_hbm, mats_hbm, out_ref, inv_ref,
    s_ref, w_ref, g_ref, twist, mats, halo_out, halo_in, cols_buf, gated, f0_buf, mix_buf, h_in, x_in, y_out, y_in,
    sum_out, sum_in, spec_buf, filt_buf,
    halo_sem, h_send, h_recv, x_send, x_recv, y_send, y_recv, sum_send, sum_recv, own_sem,
    load_sem,
):
    n, group, width = gated.shape
    part = group // chunks
    rows = math.gcd(part, 32)
    chans = n * group
    cores = sum_in.shape[0]
    me = lax.axis_index("seq")
    core = lax.axis_index("chan")
    mesh_id = pl.DeviceIdType.MESH

    loads = [
        pltpu.make_async_copy(src, dst, load_sem.at[i])
        for i, (src, dst) in enumerate(
            [(s_hbm, s_ref), (w_hbm, w_ref), (g_hbm, g_ref), (twist_hbm, twist), (mats_hbm, mats)]
        )
    ]
    for copy in loads:
        copy.start()

    barrier = pltpu.get_barrier_semaphore()

    def greet(o, carry):
        peer = lax.rem(me + o, n)
        pl.semaphore_signal(barrier, inc=1, device_id={"seq": peer}, device_id_type=mesh_id)
        return carry

    lax.fori_loop(1, n, greet, 0)
    for o in range(1, cores):
        pl.semaphore_signal(
            barrier, inc=1, device_id={"chan": lax.rem(core + o, cores)}, device_id_type=mesh_id
        )

    def sent(src, dst, send, recv, o, span):
        peer = lax.rem(me + o, n)
        return pltpu.make_async_remote_copy(
            src_ref=src.at[peer, span], dst_ref=dst.at[me, span],
            send_sem=send, recv_sem=recv,
            device_id={"seq": peer}, device_id_type=mesh_id,
        )

    everything = pl.ds(0, group)

    def send_h(o):
        return sent(h_ref, h_in, h_send.at[o], h_recv.at[o], o, everything)

    def send_x(c, o):
        return sent(gated, x_in, x_send.at[c, o], x_recv.at[c, o], o, pl.ds(c * part, part))

    def start_all(make, first, end):
        def body(o, carry):
            make(o).start()
            return carry

        lax.fori_loop(first, end, body, 0)

    row = lax.broadcasted_iota(jnp.int32, (16, width), 0)
    lane = lax.broadcasted_iota(jnp.int32, (16, width), 1)
    last = None
    loads[0].wait()
    for s in range(3):
        for top in range(2):
            first = 8 * top + 2 + 2 * s
            pick = ((row == first) & (lane == width - 2)) | ((row == first + 1) & (lane == width - 1))
            got = lax.dot_general(
                jnp.where(pick, 1.0, 0.0).astype(jnp.bfloat16),
                s_ref[s, top * chans // 2 : (top + 1) * chans // 2],
                (((1,), (1,)), ((), ())),
                preferred_element_type=jnp.float32,
            )
            last = got if last is None else last + got
    halo_out[...] = last.astype(jnp.bfloat16)

    halo = pltpu.make_async_remote_copy(
        src_ref=halo_out, dst_ref=halo_in, send_sem=halo_sem.at[0], recv_sem=halo_sem.at[1],
        device_id={"seq": lax.rem(me + 1, n)}, device_id_type=mesh_id,
    )
    pl.semaphore_wait(barrier, n - 1 + cores - 1)

    @pl.when(me < n - 1)
    def _():
        halo.start()

    start_all(send_h, 1, 1 + n // 2)
    start_all(send_h, 1 + n // 2, n)
    own_h = pltpu.make_async_copy(h_ref.at[me], h_in.at[me], own_sem.at[0])
    own_h.start()
    loads[1].wait()
    loads[2].wait()
    @pl.when(me > 0)
    def _():
        halo.wait_recv()

    for s in range(3):
        cols_buf[3 * s : 3 * s + 3, :] = w_ref[s]
    cols_buf[9:10, :] = g_ref[...]
    before = jnp.where(me > 0, halo_in[...].astype(jnp.float32), 0.0)
    cols_buf[10:16, : chans // 2] = before[2:8]
    cols_buf[10:16, chans // 2 :] = before[10:16]

    tall = math.gcd(chans, 256)
    per = tall // group if tall > group else 1
    steps = chans // tall
    sub = tall
    lanes = lax.broadcasted_iota(jnp.int32, (sub, width), 1)

    source = lax.broadcasted_iota(jnp.int32, (width, 2 * width), 0)
    target = lax.broadcasted_iota(jnp.int32, (width, 2 * width), 1)
    moves = (target == source + 1) & (target < width)
    moves = moves | (target == source + width + 2)
    shift = jnp.where(moves, 1.0, 0.0).astype(jnp.bfloat16)

    def feature(step, carry):
        block = lax.rem(me // per + step, steps)
        begin = pl.multiple_of(block * tall, tall)
        columns = cols_buf[:, pl.ds(begin, tall)].T
        parts = []
        for r in range(0, tall, sub):
            cols = columns[r : r + sub]
            here = pl.ds(begin + r, sub)
            made = []
            for s in range(3):
                x = s_ref[s, here, :].astype(jnp.float32)
                moved = jnp.dot(s_ref[s, here, :], shift, preferred_element_type=jnp.float32)
                one = jnp.where(lanes == 0, column(cols, 11 + 2 * s), moved[:, :width])
                two = jnp.where(lanes == 0, column(cols, 10 + 2 * s), moved[:, width:])
                two = jnp.where(lanes == 1, column(cols, 11 + 2 * s), two)
                made.append(
                    column(cols, 3 * s) * x
                    + column(cols, 3 * s + 1) * one
                    + column(cols, 3 * s + 2) * two
                )
            g = (made[1] * made[2]).astype(jnp.bfloat16)
            f0_buf[here, :] = made[0]
            mix_buf[here, :] = made[0] * (column(cols, 9) * g.astype(jnp.float32))
            if per == 1:
                gated[block, r : r + sub, :] = g
            else:
                parts.append(g.astype(jnp.float32))
        for q in range(per):
            peer = block * per + q
            if per > 1:
                begin = q * group % sub
                piece = parts[q * group // sub][begin : begin + group]
                gated[peer] = piece.astype(jnp.bfloat16)
            o = lax.rem(peer - me + n, n)

            @pl.when(o > 0)
            def _():
                send_x(0, o).start()

        return carry

    lax.fori_loop(1, steps + 1, feature, 0)
    for c in range(1, chunks):
        start_all(functools.partial(send_x, c), 1, n)
    own_x = pltpu.make_async_copy(gated.at[me], x_in.at[me], own_sem.at[1])
    own_x.start()
    own_h.wait()
    loads[3].wait()
    loads[4].wait()

    def wait_all(make):
        def body(o, carry):
            make(o).wait()
            return carry

        lax.fori_loop(1, n, body, 0)

    wait_all(send_h)

    def filter_rows(r, carry):
        begin = pl.multiple_of(r * rows, rows)

        def load(a):
            return h_in[a, pl.ds(begin, rows), :]

        filt_buf[r] = forward(load, twist, mats, spec_buf, n, rows, width)
        return carry

    lax.fori_loop(0, group // rows, filter_rows, 0)
    own_x.wait()

    def send_y(c, o):
        span = pl.ds(c * part, part)
        return sent(y_out, y_in, y_send.at[c, o], y_recv.at[c, o], o, span)

    def conv_rows(r, carry):
        begin = pl.multiple_of(r * rows, rows)

        def load(a):
            return x_in[a, pl.ds(begin, rows), :]

        def store(a, value):
            y_out[a, pl.ds(begin, rows), :] = value

        fx = forward(load, twist, mats, spec_buf, n, rows, width)
        xr, xi = fx[:, :width], fx[:, width:]
        hr, hi = filt_buf[r, :, :width], filt_buf[r, :, width:]
        prod = jnp.concatenate([xr * hr - xi * hi, xr * hi + xi * hr], axis=1)
        backward(prod, store, twist, mats, spec_buf, n, rows, width)
        return carry

    own_y = []
    per_chunk = part // rows
    for c in range(chunks):
        wait_all(functools.partial(send_x, c))
        lax.fori_loop(c * per_chunk, (c + 1) * per_chunk, conv_rows, 0)
        start_all(functools.partial(send_y, c), 1, n)
        span = pl.ds(c * part, part)
        own_y.append(
            pltpu.make_async_copy(y_out.at[me, span], y_in.at[me, span], own_sem.at[2 + c])
        )
        own_y[c].start()

    sum_out[...] = jnp.zeros_like(sum_out)
    for c in range(chunks):

        def mix(source):
            begin = pl.multiple_of(source * group + c * part, part)
            y = y_in[source, pl.ds(c * part, part), :].astype(jnp.float32)
            mixed = f0_buf[pl.ds(begin, part), :] * y + mix_buf[pl.ds(begin, part), :]
            out_ref[pl.ds(begin, part), :] = mixed.astype(jnp.float32)
            sum_out[...] += jnp.sum((mixed * mixed).reshape(part // 8, 8, width), axis=0)

        own_y[c].wait()
        mix(me)

        def finish(o, carry):
            send_y(c, o).wait()
            mix(lax.rem(me - o + n, n))
            return carry

        lax.fori_loop(1, n, finish, 0)

    shared = []
    for o in range(1, cores):
        shared.append(
            pltpu.make_async_remote_copy(
                src_ref=sum_out, dst_ref=sum_in.at[core],
                send_sem=sum_send.at[o], recv_sem=sum_recv.at[o],
                device_id={"chan": lax.rem(core + o, cores)}, device_id_type=mesh_id,
            )
        )
        shared[-1].start()
    total = sum_out[...]
    for o in range(1, cores):
        shared[o - 1].wait()
        total = total + sum_in[lax.rem(core - o + cores, cores)]
    total = jnp.sum(total, axis=0, keepdims=True)
    inv_rms = lax.rsqrt(total / C + EPS)

    inv_ref[...] = inv_rms

    @pl.when(me < n - 1)
    def _():
        halo.wait_send()


CHUNKS = 2


def local(streams, feat_weights, skip_gain, filter_taps):
    n, cores = lax.axis_size("seq"), lax.axis_size("chan")
    chans, width = filter_taps.shape
    group = chans // n
    chunks = CHUNKS if group % (16 * CHUNKS) == 0 else 1
    rows = math.gcd(group // chunks, 32)
    twist, mats = tables(n, width)
    vmem = pl.BlockSpec(memory_space=pltpu.VMEM)
    dma = pltpu.SemaphoreType.DMA
    half = pltpu.VMEM((n, group, width), jnp.bfloat16)
    whole = pltpu.VMEM((chans, width), jnp.float32)
    mixed, inv = pl.pallas_call(
        functools.partial(fused_kernel, chunks),
        in_specs=[pl.BlockSpec(memory_space=pl.ANY)] * 6,
        out_specs=[vmem, vmem],
        out_shape=[pltpu.VMEM((chans, width), jnp.float32), pltpu.VMEM((1, width), jnp.float32)],
        scratch_shapes=[
            pltpu.VMEM(streams.shape, jnp.bfloat16),
            pltpu.VMEM((3, TAPS, chans), jnp.float32),
            pltpu.VMEM((1, chans), jnp.float32),
            pltpu.VMEM(twist.shape, jnp.float32),
            pltpu.VMEM(mats.shape, jnp.bfloat16),
            pltpu.VMEM((16, chans // 2), jnp.bfloat16),
            pltpu.VMEM((16, chans // 2), jnp.bfloat16),
            pltpu.VMEM((16, chans), jnp.float32),
            half, whole, whole, half, half, half, half,
            pltpu.VMEM((8, width), jnp.float32),
            pltpu.VMEM((cores, 8, width), jnp.float32),
            pltpu.VMEM((n + 1, rows, 2 * width), jnp.float32),
            pltpu.VMEM((group // rows, (n + 1) * rows, 2 * width), jnp.float32),
            dma((2,)),
            dma((n,)), dma((n,)), dma((chunks, n)), dma((chunks, n)),
            dma((chunks, n)), dma((chunks, n)),
            dma((cores,)), dma((cores,)), dma((2 + chunks,)), dma((5,)),
        ],
        compiler_params=pltpu.CompilerParams(
            collective_id=0, has_side_effects=True, vmem_limit_bytes=60 << 20
        ),
    )(
        streams, feat_weights.transpose(0, 2, 1), skip_gain[None, :],
        filter_taps.reshape(n, group, width), jnp.asarray(twist), jnp.asarray(mats),
    )
    return (mixed.astype(jnp.float32) * inv).astype(jnp.bfloat16)


def solution(mesh):
    placed = (P(None, "chan", "seq"), P(None, "chan", None), P("chan"), P("chan", "seq"))
    return jax.shard_map(
        local, mesh=mesh, in_specs=placed, out_specs=P("chan", "seq"), check_vma=False
    )
```

```python
import functools
import math

import jax
import jax.numpy as jnp
import numpy as np
from jax import lax
from jax.experimental import pallas as pl
from jax.experimental.pallas import tpu as pltpu
from jax.sharding import PartitionSpec as P

C = 4096
TAPS = 3
EPS = 1e-05


def add(a, b):
    if a is None:
        return b
    return a if b is None else a + b


def sub(a, b):
    if b is None:
        return a
    return -b if a is None else a - b


def times(pair, angle):
    re, im = pair
    c, s = math.cos(angle), math.sin(angle)
    if abs(s) < 1e-12 and c > 0:
        return pair
    if abs(c) < 1e-12:
        turned = (None if im is None else -im, re)
        return turned if s > 0 else (None if turned[0] is None else -turned[0], -re)
    if im is None:
        return (re * c, re * s)
    return (re * c - im * s, re * s + im * c)


def real_fft(xs, n):
    if n == 2:
        return [(xs[0], None), (xs[0], None)]
    even = real_fft(xs[0::2], n // 2)
    odd = real_fft(xs[1::2], n // 2)
    out = [None] * (n // 2 + 1)
    for k in range(n // 4 + 1):
        er, ei = even[k]
        tr, ti = times(odd[k], -2.0 * math.pi * k / n)
        out[k] = (add(er, tr), add(ei, ti))
        if n // 2 - k != k:
            out[n // 2 - k] = (sub(er, tr), sub(ti, ei))
    return out


def real_ifft(spec, n):
    if n == 2:
        return [spec[0][0] + spec[1][0]]
    even, odd = [], []
    for k in range(n // 4 + 1):
        ar, ai = spec[k]
        br, bi = spec[n // 2 - k]
        if n // 2 - k == k:
            er, ei, dr, di = ar + ar, None, None, add(ai, ai)
            even.append((er, ei))
            odd.append((-di if di is not None else None, None))
            continue
        even.append((ar + br, sub(ai, bi)))
        odd.append(times((ar - br, add(ai, bi)), 2.0 * math.pi * k / n))
    first = real_ifft(even, n // 2)
    second = real_ifft(odd, n // 2)
    out = []
    for a, b in zip(first, second):
        out += [a, b]
    return out


def tables(blocks, width):
    total = 2 * blocks * width
    k1 = np.arange(blocks + 1)[:, None]
    i = np.arange(width)[None, :]
    ang = 2.0 * np.pi * ((k1 * i) % total) / total
    twist = np.stack([np.cos(ang), np.sin(ang)]).astype(np.float32)[:, :, None, :]
    j = np.arange(width)
    ang = 2.0 * np.pi * ((j[:, None] * j[None, :]) % width) / width
    c, s = np.cos(ang), np.sin(ang)
    forward = np.block([[c, -s], [s, c]])
    inverse = np.block([[c, s], [-s, c]]) / total
    out = []
    for m in (forward, inverse):
        hi = m.astype(np.float32).astype(jnp.bfloat16)
        lo = (m - hi.astype(np.float64)).astype(np.float32).astype(jnp.bfloat16)
        out += [hi, lo]
    return twist, np.stack(out)


def split_dot(x, hi_w, lo_w):
    hi = x.astype(jnp.bfloat16)
    lo = (x - hi.astype(jnp.float32)).astype(jnp.bfloat16)
    dot = functools.partial(jnp.dot, preferred_element_type=jnp.float32)
    return dot(hi, hi_w) + (dot(lo, hi_w) + dot(hi, lo_w))


def forward(load, twist, mats, buf, blocks, rows, width):
    xs = [load(a).astype(jnp.float32) for a in range(blocks)]
    for k, (re, im) in enumerate(real_fft(xs, 2 * blocks)):
        tc, ts = twist[0, k], twist[1, k]
        if k == 0:
            new_re, new_im = re, jnp.zeros_like(re)
        elif im is None:
            new_re, new_im = re * tc, -(re * ts)
        else:
            new_re, new_im = re * tc + im * ts, im * tc - re * ts
        buf[k, :, :width] = new_re
        buf[k, :, width:] = new_im
    flat = (blocks + 1) * rows
    return split_dot(buf[...].reshape(flat, 2 * width), mats[0], mats[1])


def backward(prod, store, twist, mats, buf, blocks, rows, width):
    back = split_dot(prod, mats[2], mats[3])
    buf[...] = back.reshape(blocks + 1, rows, 2 * width)
    spec = []
    for k in range(blocks + 1):
        re, im = buf[k, :, :width], buf[k, :, width:]
        tc, ts = twist[0, k], twist[1, k]
        out_re = re if k == 0 else re * tc - im * ts
        out_im = None if k in (0, blocks) else re * ts + im * tc
        spec.append((out_re, out_im))
    for a, y in enumerate(real_ifft(spec, 2 * blocks)):
        store(a, y.astype(jnp.bfloat16))


def column(cols, j):
    return cols[:, j : j + 1]


def fused_kernel(
    chunks, s_hbm, w_hbm, g_hbm, h_ref, twist_hbm, mats_hbm, out_ref, inv_ref,
    s_ref, w_ref, g_ref, twist, mats, halo_out, halo_in, cols_buf, gated, f0_buf, mix_buf, h_in, x_in, y_out, y_in,
    sum_out, sum_in, spec_buf, filt_buf,
    halo_sem, h_send, h_recv, x_send, x_recv, y_send, y_recv, sum_send, sum_recv, own_sem,
    load_sem,
):
    n, group, width = gated.shape
    part = group // chunks
    rows = math.gcd(part, 32)
    chans = n * group
    cores = sum_in.shape[0]
    me = lax.axis_index("seq")
    core = lax.axis_index("chan")
    mesh_id = pl.DeviceIdType.MESH

    loads = [
        pltpu.make_async_copy(src, dst, load_sem.at[i])
        for i, (src, dst) in enumerate(
            [(s_hbm, s_ref), (w_hbm, w_ref), (g_hbm, g_ref), (twist_hbm, twist), (mats_hbm, mats)]
        )
    ]
    for copy in loads:
        copy.start()

    barrier = pltpu.get_barrier_semaphore()

    def greet(o, carry):
        peer = lax.rem(me + o, n)
        pl.semaphore_signal(barrier, inc=1, device_id={"seq": peer}, device_id_type=mesh_id)
        return carry

    lax.fori_loop(1, n, greet, 0)
    for o in range(1, cores):
        pl.semaphore_signal(
            barrier, inc=1, device_id={"chan": lax.rem(core + o, cores)}, device_id_type=mesh_id
        )

    def sent(src, dst, send, recv, o, span):
        peer = lax.rem(me + o, n)
        return pltpu.make_async_remote_copy(
            src_ref=src.at[peer, span], dst_ref=dst.at[me, span],
            send_sem=send, recv_sem=recv,
            device_id={"seq": peer}, device_id_type=mesh_id,
        )

    everything = pl.ds(0, group)

    def send_h(o):
        return sent(h_ref, h_in, h_send, h_recv, o, everything)

    def send_x(c, o):
        return sent(gated, x_in, x_send, x_recv.at[c], o, pl.ds(c * part, part))

    def start_all(make, first, end):
        def body(o, carry):
            make(o).start()
            return carry

        lax.fori_loop(first, end, body, 0, unroll=True)

    row = lax.broadcasted_iota(jnp.int32, (16, width), 0)
    lane = lax.broadcasted_iota(jnp.int32, (16, width), 1)
    last = None
    loads[0].wait()
    for s in range(3):
        for top in range(2):
            first = 8 * top + 2 + 2 * s
            pick = ((row == first) & (lane == width - 2)) | ((row == first + 1) & (lane == width - 1))
            got = lax.dot_general(
                jnp.where(pick, 1.0, 0.0).astype(jnp.bfloat16),
                s_ref[s, top * chans // 2 : (top + 1) * chans // 2],
                (((1,), (1,)), ((), ())),
                preferred_element_type=jnp.float32,
            )
            last = got if last is None else last + got
    halo_out[...] = last.astype(jnp.bfloat16)

    halo = pltpu.make_async_remote_copy(
        src_ref=halo_out, dst_ref=halo_in, send_sem=halo_sem.at[0], recv_sem=halo_sem.at[1],
        device_id={"seq": lax.rem(me + 1, n)}, device_id_type=mesh_id,
    )
    pl.semaphore_wait(barrier, n - 1 + cores - 1)

    @pl.when(me < n - 1)
    def _():
        halo.start()

    start_all(send_h, 1, 1 + n // 2)
    start_all(send_h, 1 + n // 2, n)
    own_h = pltpu.make_async_copy(h_ref.at[me], h_in.at[me], own_sem.at[0])
    own_h.start()
    loads[1].wait()
    loads[2].wait()
    @pl.when(me > 0)
    def _():
        halo.wait_recv()

    for s in range(3):
        cols_buf[3 * s : 3 * s + 3, :] = w_ref[s]
    cols_buf[9:10, :] = g_ref[...]
    before = jnp.where(me > 0, halo_in[...].astype(jnp.float32), 0.0)
    cols_buf[10:16, : chans // 2] = before[2:8]
    cols_buf[10:16, chans // 2 :] = before[10:16]

    tall = math.gcd(chans, 256)
    per = tall // group if tall > group else 1
    steps = chans // tall
    sub = tall
    lanes = lax.broadcasted_iota(jnp.int32, (sub, width), 1)

    source = lax.broadcasted_iota(jnp.int32, (width, 2 * width), 0)
    target = lax.broadcasted_iota(jnp.int32, (width, 2 * width), 1)
    moves = (target == source + 1) & (target < width)
    moves = moves | (target == source + width + 2)
    shift = jnp.where(moves, 1.0, 0.0).astype(jnp.bfloat16)

    def feature(step, carry):
        block = lax.rem(me // per + step, steps)
        begin = pl.multiple_of(block * tall, tall)
        columns = cols_buf[:, pl.ds(begin, tall)].T
        parts = []
        for r in range(0, tall, sub):
            cols = columns[r : r + sub]
            here = pl.ds(begin + r, sub)
            made = []
            for s in range(3):
                x = s_ref[s, here, :].astype(jnp.float32)
                moved = jnp.dot(s_ref[s, here, :], shift, preferred_element_type=jnp.float32)
                one = jnp.where(lanes == 0, column(cols, 11 + 2 * s), moved[:, :width])
                two = jnp.where(lanes == 0, column(cols, 10 + 2 * s), moved[:, width:])
                two = jnp.where(lanes == 1, column(cols, 11 + 2 * s), two)
                made.append(
                    column(cols, 3 * s) * x
                    + column(cols, 3 * s + 1) * one
                    + column(cols, 3 * s + 2) * two
                )
            g = (made[1] * made[2]).astype(jnp.bfloat16)
            f0_buf[here, :] = made[0]
            mix_buf[here, :] = made[0] * (column(cols, 9) * g.astype(jnp.float32))
            if per == 1:
                gated[block, r : r + sub, :] = g
            else:
                parts.append(g.astype(jnp.float32))
        for q in range(per):
            peer = block * per + q
            if per > 1:
                begin = q * group % sub
                piece = parts[q * group // sub][begin : begin + group]
                gated[peer] = piece.astype(jnp.bfloat16)
            o = lax.rem(peer - me + n, n)

            @pl.when(o > 0)
            def _():
                send_x(0, o).start()

        return carry

    lax.fori_loop(1, steps + 1, feature, 0)
    for c in range(1, chunks):
        start_all(functools.partial(send_x, c), 1, n)
    own_x = pltpu.make_async_copy(gated.at[me], x_in.at[me], own_sem.at[1])
    own_x.start()
    own_h.wait()
    loads[3].wait()
    loads[4].wait()

    def drain(sem, count):
        some = s_ref.at[0, pl.ds(0, count)]
        pltpu.make_async_copy(some, some, sem).wait()

    drain(h_recv, (n - 1) * group)

    def filter_rows(r, carry):
        begin = pl.multiple_of(r * rows, rows)

        def load(a):
            return h_in[a, pl.ds(begin, rows), :]

        filt_buf[r] = forward(load, twist, mats, spec_buf, n, rows, width)
        return carry

    lax.fori_loop(0, group // rows, filter_rows, 0)
    own_x.wait()

    def send_y(c, o):
        span = pl.ds(c * part, part)
        return sent(y_out, y_in, y_send, y_recv.at[c], o, span)

    def conv_rows(r, carry):
        begin = pl.multiple_of(r * rows, rows)

        def load(a):
            return x_in[a, pl.ds(begin, rows), :]

        def store(a, value):
            y_out[a, pl.ds(begin, rows), :] = value

        fx = forward(load, twist, mats, spec_buf, n, rows, width)
        xr, xi = fx[:, :width], fx[:, width:]
        hr, hi = filt_buf[r, :, :width], filt_buf[r, :, width:]
        prod = jnp.concatenate([xr * hr - xi * hi, xr * hi + xi * hr], axis=1)
        backward(prod, store, twist, mats, spec_buf, n, rows, width)
        return carry

    own_y = []
    per_chunk = part // rows
    for c in range(chunks):
        drain(x_recv.at[c], (n - 1) * part)
        lax.fori_loop(c * per_chunk, (c + 1) * per_chunk, conv_rows, 0)
        start_all(functools.partial(send_y, c), 1, n)
        span = pl.ds(c * part, part)
        own_y.append(
            pltpu.make_async_copy(y_out.at[me, span], y_in.at[me, span], own_sem.at[2 + c])
        )
        own_y[c].start()

    squares = jnp.zeros_like(sum_out)
    for c in range(chunks):

        def mix(source):
            begin = pl.multiple_of(source * group + c * part, part)
            y = y_in[source, pl.ds(c * part, part), :].astype(jnp.float32)
            mixed = f0_buf[pl.ds(begin, part), :] * y + mix_buf[pl.ds(begin, part), :]
            out_ref[pl.ds(begin, part), :] = mixed.astype(jnp.float32)
            return jnp.sum((mixed * mixed).reshape(part // 8, 8, width), axis=0)

        def finish(source, carry):
            return carry + mix(source)

        own_y[c].wait()
        drain(y_recv.at[c], (n - 1) * part)
        squares = lax.fori_loop(0, n, finish, squares, unroll=2)

    sum_out[...] = squares
    shared = []
    for o in range(1, cores):
        shared.append(
            pltpu.make_async_remote_copy(
                src_ref=sum_out, dst_ref=sum_in.at[core],
                send_sem=sum_send.at[o], recv_sem=sum_recv.at[o],
                device_id={"chan": lax.rem(core + o, cores)}, device_id_type=mesh_id,
            )
        )
        shared[-1].start()
    for sem in (h_send, x_send, y_send):
        drain(sem, (n - 1) * group)
    total = sum_out[...]
    for o in range(1, cores):
        shared[o - 1].wait()
        total = total + sum_in[lax.rem(core - o + cores, cores)]
    total = jnp.sum(total, axis=0, keepdims=True)
    inv_rms = lax.rsqrt(total / C + EPS)

    inv_ref[...] = inv_rms

    @pl.when(me < n - 1)
    def _():
        halo.wait_send()


CHUNKS = 4


def local(streams, feat_weights, skip_gain, filter_taps):
    n, cores = lax.axis_size("seq"), lax.axis_size("chan")
    chans, width = filter_taps.shape
    group = chans // n
    chunks = CHUNKS if group % (16 * CHUNKS) == 0 else 1
    rows = math.gcd(group // chunks, 32)
    twist, mats = tables(n, width)
    vmem = pl.BlockSpec(memory_space=pltpu.VMEM)
    dma = pltpu.SemaphoreType.DMA
    half = pltpu.VMEM((n, group, width), jnp.bfloat16)
    whole = pltpu.VMEM((chans, width), jnp.float32)
    mixed, inv = pl.pallas_call(
        functools.partial(fused_kernel, chunks),
        in_specs=[pl.BlockSpec(memory_space=pl.ANY)] * 6,
        out_specs=[vmem, vmem],
        out_shape=[pltpu.VMEM((chans, width), jnp.float32), pltpu.VMEM((1, width), jnp.float32)],
        scratch_shapes=[
            pltpu.VMEM(streams.shape, jnp.bfloat16),
            pltpu.VMEM((3, TAPS, chans), jnp.float32),
            pltpu.VMEM((1, chans), jnp.float32),
            pltpu.VMEM(twist.shape, jnp.float32),
            pltpu.VMEM(mats.shape, jnp.bfloat16),
            pltpu.VMEM((16, chans // 2), jnp.bfloat16),
            pltpu.VMEM((16, chans // 2), jnp.bfloat16),
            pltpu.VMEM((16, chans), jnp.float32),
            half, whole, whole, half, half, half, half,
            pltpu.VMEM((8, width), jnp.float32),
            pltpu.VMEM((cores, 8, width), jnp.float32),
            pltpu.VMEM((n + 1, rows, 2 * width), jnp.float32),
            pltpu.VMEM((group // rows, (n + 1) * rows, 2 * width), jnp.float32),
            dma((2,)),
            dma(()), dma(()), dma(()), dma((chunks,)),
            dma(()), dma((chunks,)),
            dma((cores,)), dma((cores,)), dma((2 + chunks,)), dma((5,)),
        ],
        compiler_params=pltpu.CompilerParams(
            collective_id=0, has_side_effects=True, vmem_limit_bytes=60 << 20
        ),
    )(
        streams, feat_weights.transpose(0, 2, 1), skip_gain[None, :],
        filter_taps.reshape(n, group, width), jnp.asarray(twist), jnp.asarray(mats),
    )
    return (mixed.astype(jnp.float32) * inv).astype(jnp.bfloat16)


def solution(mesh):
    placed = (P(None, "chan", "seq"), P(None, "chan", None), P("chan"), P("chan", "seq"))
    return jax.shard_map(
        local, mesh=mesh, in_specs=placed, out_specs=P("chan", "seq"), check_vma=False
    )
```

```python
import functools
import math

import jax
import jax.numpy as jnp
import numpy as np
from jax import lax
from jax.experimental import pallas as pl
from jax.experimental.pallas import tpu as pltpu
from jax.sharding import PartitionSpec as P

C = 4096
TAPS = 3
EPS = 1e-05


def add(a, b):
    if a is None:
        return b
    return a if b is None else a + b


def sub(a, b):
    if b is None:
        return a
    return -b if a is None else a - b


def times(pair, angle):
    re, im = pair
    c, s = math.cos(angle), math.sin(angle)
    if abs(s) < 1e-12 and c > 0:
        return pair
    if abs(c) < 1e-12:
        turned = (None if im is None else -im, re)
        return turned if s > 0 else (None if turned[0] is None else -turned[0], -re)
    if im is None:
        return (re * c, re * s)
    return (re * c - im * s, re * s + im * c)


def real_fft(xs, n):
    if n == 2:
        return [(xs[0], None), (xs[0], None)]
    even = real_fft(xs[0::2], n // 2)
    odd = real_fft(xs[1::2], n // 2)
    out = [None] * (n // 2 + 1)
    for k in range(n // 4 + 1):
        er, ei = even[k]
        tr, ti = times(odd[k], -2.0 * math.pi * k / n)
        out[k] = (add(er, tr), add(ei, ti))
        if n // 2 - k != k:
            out[n // 2 - k] = (sub(er, tr), sub(ti, ei))
    return out


def real_ifft(spec, n):
    if n == 2:
        return [spec[0][0] + spec[1][0]]
    even, odd = [], []
    for k in range(n // 4 + 1):
        ar, ai = spec[k]
        br, bi = spec[n // 2 - k]
        if n // 2 - k == k:
            er, ei, dr, di = ar + ar, None, None, add(ai, ai)
            even.append((er, ei))
            odd.append((-di if di is not None else None, None))
            continue
        even.append((ar + br, sub(ai, bi)))
        odd.append(times((ar - br, add(ai, bi)), 2.0 * math.pi * k / n))
    first = real_ifft(even, n // 2)
    second = real_ifft(odd, n // 2)
    out = []
    for a, b in zip(first, second):
        out += [a, b]
    return out


def tables(blocks, width):
    total = 2 * blocks * width
    k1 = np.arange(blocks + 1)[:, None]
    i = np.arange(width)[None, :]
    ang = 2.0 * np.pi * ((k1 * i) % total) / total
    twist = np.stack([np.cos(ang), np.sin(ang)]).astype(np.float32)[:, :, None, :]
    j = np.arange(width)
    ang = 2.0 * np.pi * ((j[:, None] * j[None, :]) % width) / width
    c, s = np.cos(ang), np.sin(ang)
    forward = np.block([[c, -s], [s, c]])
    inverse = np.block([[c, s], [-s, c]]) / total
    out = []
    for m in (forward, inverse):
        hi = m.astype(np.float32).astype(jnp.bfloat16)
        lo = (m - hi.astype(np.float64)).astype(np.float32).astype(jnp.bfloat16)
        out += [hi, lo]
    return twist, np.stack(out)


def split_dot(x, hi_w, lo_w):
    hi = x.astype(jnp.bfloat16)
    lo = (x - hi.astype(jnp.float32)).astype(jnp.bfloat16)
    dot = functools.partial(jnp.dot, preferred_element_type=jnp.float32)
    return dot(hi, hi_w) + (dot(lo, hi_w) + dot(hi, lo_w))


def forward(load, twist, mats, buf, blocks, rows, width):
    xs = [load(a).astype(jnp.float32) for a in range(blocks)]
    for k, (re, im) in enumerate(real_fft(xs, 2 * blocks)):
        tc, ts = twist[0, k], twist[1, k]
        if k == 0:
            new_re, new_im = re, jnp.zeros_like(re)
        elif im is None:
            new_re, new_im = re * tc, -(re * ts)
        else:
            new_re, new_im = re * tc + im * ts, im * tc - re * ts
        buf[k, :, :width] = new_re
        buf[k, :, width:] = new_im
    flat = (blocks + 1) * rows
    return split_dot(buf[...].reshape(flat, 2 * width), mats[0], mats[1])


def backward(prod, store, twist, mats, buf, blocks, rows, width):
    back = split_dot(prod, mats[2], mats[3])
    buf[...] = back.reshape(blocks + 1, rows, 2 * width)
    spec = []
    for k in range(blocks + 1):
        re, im = buf[k, :, :width], buf[k, :, width:]
        tc, ts = twist[0, k], twist[1, k]
        out_re = re if k == 0 else re * tc - im * ts
        out_im = None if k in (0, blocks) else re * ts + im * tc
        spec.append((out_re, out_im))
    for a, y in enumerate(real_ifft(spec, 2 * blocks)):
        store(a, y.astype(jnp.bfloat16))


def column(cols, j):
    return cols[:, j : j + 1]


def fused_kernel(
    chunks, s_hbm, w_hbm, g_hbm, h_ref, twist_hbm, mats_hbm, out_ref, inv_ref,
    s_ref, w_ref, g_ref, twist, mats, halo_out, halo_in, cols_buf, gated, f0_buf, mix_buf, h_in, x_in, y_out, y_in,
    sum_out, sum_in, spec_buf, filt_buf,
    halo_sem, h_send, h_recv, x_send, x_recv, y_send, y_recv, sum_send, sum_recv, own_sem,
    load_sem,
):
    n, group, width = gated.shape
    part = group // chunks
    rows = math.gcd(part, 32)
    chans = n * group
    cores = sum_in.shape[0]
    me = lax.axis_index("seq")
    core = lax.axis_index("chan")
    mesh_id = pl.DeviceIdType.MESH

    loads = [
        pltpu.make_async_copy(src, dst, load_sem.at[i])
        for i, (src, dst) in enumerate(
            [(s_hbm, s_ref), (w_hbm, w_ref), (g_hbm, g_ref), (twist_hbm, twist), (mats_hbm, mats)]
        )
    ]
    for copy in loads:
        copy.start()

    barrier = pltpu.get_barrier_semaphore()

    def greet(o, carry):
        peer = lax.rem(me + o, n)
        pl.semaphore_signal(barrier, inc=1, device_id={"seq": peer}, device_id_type=mesh_id)
        return carry

    lax.fori_loop(1, n, greet, 0)
    for o in range(1, cores):
        pl.semaphore_signal(
            barrier, inc=1, device_id={"chan": lax.rem(core + o, cores)}, device_id_type=mesh_id
        )

    def sent(src, dst, send, recv, o, span):
        peer = lax.rem(me + o, n)
        return pltpu.make_async_remote_copy(
            src_ref=src.at[peer, span], dst_ref=dst.at[me, span],
            send_sem=send, recv_sem=recv,
            device_id={"seq": peer}, device_id_type=mesh_id,
        )

    everything = pl.ds(0, group)

    def send_h(o):
        return sent(h_ref, h_in, h_send, h_recv, jnp.where(o <= n // 2, (1 - me // (n // 2)) * (n // 2) + lax.rem(me + o - 1, n // 2), me // (n // 2) * (n // 2) + lax.rem(me + o - n // 2, n // 2)) - me + n, everything)

    def send_x(c, o):
        return sent(gated, x_in, x_send, x_recv.at[c], o, pl.ds(c * part, part))

    def start_all(make, first, end):
        def body(o, carry):
            make(o).start()
            return carry

        lax.fori_loop(first, end, body, 0, unroll=True)

    row = lax.broadcasted_iota(jnp.int32, (16, width), 0)
    lane = lax.broadcasted_iota(jnp.int32, (16, width), 1)
    last = None
    loads[0].wait()
    for s in range(3):
        for top in range(2):
            first = 8 * top + 2 + 2 * s
            pick = ((row == first) & (lane == width - 2)) | ((row == first + 1) & (lane == width - 1))
            got = lax.dot_general(
                jnp.where(pick, 1.0, 0.0).astype(jnp.bfloat16),
                s_ref[s, top * chans // 2 : (top + 1) * chans // 2],
                (((1,), (1,)), ((), ())),
                preferred_element_type=jnp.float32,
            )
            last = got if last is None else last + got
    halo_out[...] = last.astype(jnp.bfloat16)

    halo = pltpu.make_async_remote_copy(
        src_ref=halo_out, dst_ref=halo_in, send_sem=halo_sem.at[0], recv_sem=halo_sem.at[1],
        device_id={"seq": lax.rem(me + 1, n)}, device_id_type=mesh_id,
    )
    pl.semaphore_wait(barrier, n - 1 + cores - 1)

    @pl.when(me < n - 1)
    def _():
        halo.start()

    start_all(send_h, 1, 1 + n // 2)
    start_all(send_h, 1 + n // 2, n)
    own_h = pltpu.make_async_copy(h_ref.at[me], h_in.at[me], own_sem.at[0])
    own_h.start()
    loads[1].wait()
    loads[2].wait()
    @pl.when(me > 0)
    def _():
        halo.wait_recv()

    for s in range(3):
        cols_buf[3 * s : 3 * s + 3, :] = w_ref[s]
    cols_buf[9:10, :] = g_ref[...]
    before = jnp.where(me > 0, halo_in[...].astype(jnp.float32), 0.0)
    cols_buf[10:16, : chans // 2] = before[2:8]
    cols_buf[10:16, chans // 2 :] = before[10:16]

    tall = math.gcd(chans, 256)
    per = tall // group if tall > group else 1
    steps = chans // tall
    sub = tall
    lanes = lax.broadcasted_iota(jnp.int32, (sub, width), 1)

    source = lax.broadcasted_iota(jnp.int32, (width, 2 * width), 0)
    target = lax.broadcasted_iota(jnp.int32, (width, 2 * width), 1)
    moves = (target == source + 1) & (target < width)
    moves = moves | (target == source + width + 2)
    shift = jnp.where(moves, 1.0, 0.0).astype(jnp.bfloat16)

    def feature(step, carry):
        block = lax.rem(me // per + step, steps)
        begin = pl.multiple_of(block * tall, tall)
        columns = cols_buf[:, pl.ds(begin, tall)].T
        parts = []
        for r in range(0, tall, sub):
            cols = columns[r : r + sub]
            here = pl.ds(begin + r, sub)
            made = []
            for s in range(3):
                x = s_ref[s, here, :].astype(jnp.float32)
                moved = jnp.dot(s_ref[s, here, :], shift, preferred_element_type=jnp.float32)
                one = jnp.where(lanes == 0, column(cols, 11 + 2 * s), moved[:, :width])
                two = jnp.where(lanes == 0, column(cols, 10 + 2 * s), moved[:, width:])
                two = jnp.where(lanes == 1, column(cols, 11 + 2 * s), two)
                made.append(
                    column(cols, 3 * s) * x
                    + column(cols, 3 * s + 1) * one
                    + column(cols, 3 * s + 2) * two
                )
            g = (made[1] * made[2]).astype(jnp.bfloat16)
            f0_buf[here, :] = made[0]
            mix_buf[here, :] = made[0] * (column(cols, 9) * g.astype(jnp.float32))
            if per == 1:
                gated[block, r : r + sub, :] = g
            else:
                parts.append(g.astype(jnp.float32))
        for q in range(per):
            peer = block * per + q
            if per > 1:
                begin = q * group % sub
                piece = parts[q * group // sub][begin : begin + group]
                gated[peer] = piece.astype(jnp.bfloat16)
            o = lax.rem(peer - me + n, n)

            @pl.when(o > 0)
            def _():
                send_x(0, o).start()

        return carry

    lax.fori_loop(1, steps + 1, feature, 0)
    for c in range(1, chunks):
        start_all(functools.partial(send_x, c), 1, n)
    own_x = pltpu.make_async_copy(gated.at[me], x_in.at[me], own_sem.at[1])
    own_x.start()
    own_h.wait()
    loads[3].wait()
    loads[4].wait()

    def drain(sem, count):
        some = s_ref.at[0, pl.ds(0, count)]
        pltpu.make_async_copy(some, some, sem).wait()

    drain(h_recv, (n - 1) * group)

    def filter_rows(r, carry):
        begin = pl.multiple_of(r * rows, rows)

        def load(a):
            return h_in[a, pl.ds(begin, rows), :]

        filt_buf[r] = forward(load, twist, mats, spec_buf, n, rows, width)
        return carry

    lax.fori_loop(0, group // rows, filter_rows, 0)
    own_x.wait()

    def send_y(c, o):
        span = pl.ds(c * part, part)
        return sent(y_out, y_in, y_send, y_recv.at[c], o, span)

    def conv_rows(r, carry):
        begin = pl.multiple_of(r * rows, rows)

        def load(a):
            return x_in[a, pl.ds(begin, rows), :]

        def store(a, value):
            y_out[a, pl.ds(begin, rows), :] = value

        fx = forward(load, twist, mats, spec_buf, n, rows, width)
        xr, xi = fx[:, :width], fx[:, width:]
        hr, hi = filt_buf[r, :, :width], filt_buf[r, :, width:]
        prod = jnp.concatenate([xr * hr - xi * hi, xr * hi + xi * hr], axis=1)
        backward(prod, store, twist, mats, spec_buf, n, rows, width)
        return carry

    own_y = []
    per_chunk = part // rows
    for c in range(chunks):
        drain(x_recv.at[c], (n - 1) * part)
        lax.fori_loop(c * per_chunk, (c + 1) * per_chunk, conv_rows, 0)
        start_all(functools.partial(send_y, c), 1, n)
        span = pl.ds(c * part, part)
        own_y.append(
            pltpu.make_async_copy(y_out.at[me, span], y_in.at[me, span], own_sem.at[2 + c])
        )
        own_y[c].start()

    squares = jnp.zeros_like(sum_out)
    for c in range(chunks):

        def mix(source):
            begin = pl.multiple_of(source * group + c * part, part)
            y = y_in[source, pl.ds(c * part, part), :].astype(jnp.float32)
            mixed = f0_buf[pl.ds(begin, part), :] * y + mix_buf[pl.ds(begin, part), :]
            out_ref[pl.ds(begin, part), :] = mixed.astype(jnp.float32)
            return jnp.sum((mixed * mixed).reshape(part // 8, 8, width), axis=0)

        def finish(source, carry):
            return carry + mix(source)

        own_y[c].wait()
        drain(y_recv.at[c], (n - 1) * part)
        squares = lax.fori_loop(0, n, finish, squares, unroll=2)

    sum_out[...] = squares
    shared = []
    for o in range(1, cores):
        shared.append(
            pltpu.make_async_remote_copy(
                src_ref=sum_out, dst_ref=sum_in.at[core],
                send_sem=sum_send.at[o], recv_sem=sum_recv.at[o],
                device_id={"chan": lax.rem(core + o, cores)}, device_id_type=mesh_id,
            )
        )
        shared[-1].start()
    for sem in (h_send, x_send, y_send):
        drain(sem, (n - 1) * group)
    total = sum_out[...]
    for o in range(1, cores):
        shared[o - 1].wait()
        total = total + sum_in[lax.rem(core - o + cores, cores)]
    total = jnp.sum(total, axis=0, keepdims=True)
    inv_rms = lax.rsqrt(total / C + EPS)

    inv_ref[...] = inv_rms

    @pl.when(me < n - 1)
    def _():
        halo.wait_send()


CHUNKS = 4


def local(streams, feat_weights, skip_gain, filter_taps):
    n, cores = lax.axis_size("seq"), lax.axis_size("chan")
    chans, width = filter_taps.shape
    group = chans // n
    chunks = CHUNKS if group % (16 * CHUNKS) == 0 else 1
    rows = math.gcd(group // chunks, 32)
    twist, mats = tables(n, width)
    vmem = pl.BlockSpec(memory_space=pltpu.VMEM)
    dma = pltpu.SemaphoreType.DMA
    half = pltpu.VMEM((n, group, width), jnp.bfloat16)
    whole = pltpu.VMEM((chans, width), jnp.float32)
    mixed, inv = pl.pallas_call(
        functools.partial(fused_kernel, chunks),
        in_specs=[pl.BlockSpec(memory_space=pl.ANY)] * 6,
        out_specs=[vmem, vmem],
        out_shape=[pltpu.VMEM((chans, width), jnp.float32), pltpu.VMEM((1, width), jnp.float32)],
        scratch_shapes=[
            pltpu.VMEM(streams.shape, jnp.bfloat16),
            pltpu.VMEM((3, TAPS, chans), jnp.float32),
            pltpu.VMEM((1, chans), jnp.float32),
            pltpu.VMEM(twist.shape, jnp.float32),
            pltpu.VMEM(mats.shape, jnp.bfloat16),
            pltpu.VMEM((16, chans // 2), jnp.bfloat16),
            pltpu.VMEM((16, chans // 2), jnp.bfloat16),
            pltpu.VMEM((16, chans), jnp.float32),
            half, whole, whole, half, half, half, half,
            pltpu.VMEM((8, width), jnp.float32),
            pltpu.VMEM((cores, 8, width), jnp.float32),
            pltpu.VMEM((n + 1, rows, 2 * width), jnp.float32),
            pltpu.VMEM((group // rows, (n + 1) * rows, 2 * width), jnp.float32),
            dma((2,)),
            dma(()), dma(()), dma(()), dma((chunks,)),
            dma(()), dma((chunks,)),
            dma((cores,)), dma((cores,)), dma((2 + chunks,)), dma((5,)),
        ],
        compiler_params=pltpu.CompilerParams(
            collective_id=0, has_side_effects=True, vmem_limit_bytes=60 << 20
        ),
    )(
        streams, feat_weights.transpose(0, 2, 1), skip_gain[None, :],
        filter_taps.reshape(n, group, width), jnp.asarray(twist), jnp.asarray(mats),
    )
    return (mixed.astype(jnp.float32) * inv).astype(jnp.bfloat16)


def solution(mesh):
    placed = (P(None, "chan", "seq"), P(None, "chan", None), P("chan"), P("chan", "seq"))
    return jax.shard_map(
        local, mesh=mesh, in_specs=placed, out_specs=P("chan", "seq"), check_vma=False
    )
```

```python
import functools
import math

import jax
import jax.numpy as jnp
import numpy as np
from jax import lax
from jax.experimental import pallas as pl
from jax.experimental.pallas import tpu as pltpu
from jax.sharding import PartitionSpec as P

C = 4096
TAPS = 3
EPS = 1e-05


def add(a, b):
    if a is None:
        return b
    return a if b is None else a + b


def sub(a, b):
    if b is None:
        return a
    return -b if a is None else a - b


def times(pair, angle):
    re, im = pair
    c, s = math.cos(angle), math.sin(angle)
    if abs(s) < 1e-12 and c > 0:
        return pair
    if abs(c) < 1e-12:
        turned = (None if im is None else -im, re)
        return turned if s > 0 else (None if turned[0] is None else -turned[0], -re)
    if im is None:
        return (re * c, re * s)
    return (re * c - im * s, re * s + im * c)


def real_fft(xs, n):
    if n == 2:
        return [(xs[0], None), (xs[0], None)]
    even = real_fft(xs[0::2], n // 2)
    odd = real_fft(xs[1::2], n // 2)
    out = [None] * (n // 2 + 1)
    for k in range(n // 4 + 1):
        er, ei = even[k]
        tr, ti = times(odd[k], -2.0 * math.pi * k / n)
        out[k] = (add(er, tr), add(ei, ti))
        if n // 2 - k != k:
            out[n // 2 - k] = (sub(er, tr), sub(ti, ei))
    return out


def real_ifft(spec, n):
    if n == 2:
        return [spec[0][0] + spec[1][0]]
    even, odd = [], []
    for k in range(n // 4 + 1):
        ar, ai = spec[k]
        br, bi = spec[n // 2 - k]
        if n // 2 - k == k:
            er, ei, dr, di = ar + ar, None, None, add(ai, ai)
            even.append((er, ei))
            odd.append((-di if di is not None else None, None))
            continue
        even.append((ar + br, sub(ai, bi)))
        odd.append(times((ar - br, add(ai, bi)), 2.0 * math.pi * k / n))
    first = real_ifft(even, n // 2)
    second = real_ifft(odd, n // 2)
    out = []
    for a, b in zip(first, second):
        out += [a, b]
    return out


def tables(blocks, width):
    total = 2 * blocks * width
    k1 = np.arange(blocks + 1)[:, None]
    i = np.arange(width)[None, :]
    ang = 2.0 * np.pi * ((k1 * i) % total) / total
    twist = np.stack([np.cos(ang), np.sin(ang)]).astype(np.float32)[:, :, None, :]
    j = np.arange(width)
    ang = 2.0 * np.pi * ((j[:, None] * j[None, :]) % width) / width
    c, s = np.cos(ang), np.sin(ang)
    forward = np.block([[c, -s], [s, c]])
    inverse = np.block([[c, s], [-s, c]]) / total
    out = []
    for m in (forward, inverse):
        hi = m.astype(np.float32).astype(jnp.bfloat16)
        lo = (m - hi.astype(np.float64)).astype(np.float32).astype(jnp.bfloat16)
        out += [hi, lo]
    return twist, np.stack(out)


def split_dot(x, hi_w, lo_w):
    hi = x.astype(jnp.bfloat16)
    lo = (x - hi.astype(jnp.float32)).astype(jnp.bfloat16)
    dot = functools.partial(jnp.dot, preferred_element_type=jnp.float32)
    return dot(hi, hi_w) + (dot(lo, hi_w) + dot(hi, lo_w))


def forward(load, twist, mats, buf, blocks, rows, width):
    xs = [load(a).astype(jnp.float32) for a in range(blocks)]
    for k, (re, im) in enumerate(real_fft(xs, 2 * blocks)):
        tc, ts = twist[0, k], twist[1, k]
        if k == 0:
            new_re, new_im = re, jnp.zeros_like(re)
        elif im is None:
            new_re, new_im = re * tc, -(re * ts)
        else:
            new_re, new_im = re * tc + im * ts, im * tc - re * ts
        buf[k, :, :width] = new_re
        buf[k, :, width:] = new_im
    flat = (blocks + 1) * rows
    return split_dot(buf[...].reshape(flat, 2 * width), mats[0], mats[1])


def backward(prod, store, twist, mats, buf, blocks, rows, width):
    back = split_dot(prod, mats[2], mats[3])
    buf[...] = back.reshape(blocks + 1, rows, 2 * width)
    spec = []
    for k in range(blocks + 1):
        re, im = buf[k, :, :width], buf[k, :, width:]
        tc, ts = twist[0, k], twist[1, k]
        out_re = re if k == 0 else re * tc - im * ts
        out_im = None if k in (0, blocks) else re * ts + im * tc
        spec.append((out_re, out_im))
    for a, y in enumerate(real_ifft(spec, 2 * blocks)):
        store(a, y.astype(jnp.bfloat16))


def column(cols, j):
    return cols[:, j : j + 1]


def fused_kernel(
    chunks, s_hbm, w_hbm, g_hbm, h_ref, twist_hbm, mats_hbm, out_ref, inv_ref,
    s_ref, w_ref, g_ref, twist, mats, halo_out, halo_in, cols_buf, gated, f0_buf, mix_buf, h_in, x_in, y_out, y_in,
    sum_out, sum_in, spec_buf, filt_buf,
    halo_sem, h_send, h_recv, x_send, x_recv, y_send, y_recv, sum_send, sum_recv, own_sem,
    load_sem,
):
    n, group, width = gated.shape
    part = group // chunks
    rows = math.gcd(part, 32)
    chans = n * group
    cores = sum_in.shape[0]
    me = lax.axis_index("seq")
    core = lax.axis_index("chan")
    mesh_id = pl.DeviceIdType.MESH

    loads = [
        pltpu.make_async_copy(src, dst, load_sem.at[i])
        for i, (src, dst) in enumerate(
            [(s_hbm, s_ref), (w_hbm, w_ref), (g_hbm, g_ref), (twist_hbm, twist), (mats_hbm, mats)]
        )
    ]
    for copy in loads:
        copy.start()

    barrier = pltpu.get_barrier_semaphore()

    def greet(o, carry):
        peer = lax.rem(me + o, n)
        pl.semaphore_signal(barrier, inc=1, device_id={"seq": peer}, device_id_type=mesh_id)
        return carry

    lax.fori_loop(1, n, greet, 0)
    for o in range(1, cores):
        pl.semaphore_signal(
            barrier, inc=1, device_id={"chan": lax.rem(core + o, cores)}, device_id_type=mesh_id
        )

    def sent(src, dst, send, recv, o, span):
        peer = lax.rem(me + o, n)
        return pltpu.make_async_remote_copy(
            src_ref=src.at[peer, span], dst_ref=dst.at[me, span],
            send_sem=send, recv_sem=recv,
            device_id={"seq": peer}, device_id_type=mesh_id,
        )

    everything = pl.ds(0, group)

    def send_h(o):
        return sent(h_ref, h_in, h_send, h_recv, jnp.where(o <= n // 2, (1 - me // (n // 2)) * (n // 2) + lax.rem(me + o - 1, n // 2), me // (n // 2) * (n // 2) + lax.rem(me + o - n // 2, n // 2)) - me + n, everything)

    def send_x(c, o):
        return sent(gated, x_in, x_send, x_recv.at[c], o, pl.ds(c * part, part))

    def start_all(make, first, end):
        def body(o, carry):
            make(o).start()
            return carry

        lax.fori_loop(first, end, body, 0, unroll=True)

    row = lax.broadcasted_iota(jnp.int32, (16, width), 0)
    lane = lax.broadcasted_iota(jnp.int32, (16, width), 1)
    last = None
    loads[0].wait()
    for s in range(3):
        for top in range(2):
            first = 8 * top + 2 + 2 * s
            pick = ((row == first) & (lane == width - 2)) | ((row == first + 1) & (lane == width - 1))
            got = lax.dot_general(
                jnp.where(pick, 1.0, 0.0).astype(jnp.bfloat16),
                s_ref[s, top * chans // 2 : (top + 1) * chans // 2],
                (((1,), (1,)), ((), ())),
                preferred_element_type=jnp.float32,
            )
            last = got if last is None else last + got
    halo_out[...] = last.astype(jnp.bfloat16)

    halo = pltpu.make_async_remote_copy(
        src_ref=halo_out, dst_ref=halo_in, send_sem=halo_sem.at[0], recv_sem=halo_sem.at[1],
        device_id={"seq": lax.rem(me + 1, n)}, device_id_type=mesh_id,
    )
    pl.semaphore_wait(barrier, n - 1 + cores - 1)

    @pl.when(me < n - 1)
    def _():
        halo.start()

    start_all(send_h, 1, 1 + n // 2)
    start_all(send_h, 1 + n // 2, n)
    own_h = pltpu.make_async_copy(h_ref.at[me], h_in.at[me], own_sem.at[0])
    own_h.start()
    loads[1].wait()
    loads[2].wait()
    @pl.when(me > 0)
    def _():
        halo.wait_recv()

    for s in range(3):
        cols_buf[3 * s : 3 * s + 3, :] = w_ref[s]
    cols_buf[9:10, :] = g_ref[...]
    before = jnp.where(me > 0, halo_in[...].astype(jnp.float32), 0.0)
    cols_buf[10:16, : chans // 2] = before[2:8]
    cols_buf[10:16, chans // 2 :] = before[10:16]

    tall = math.gcd(chans, 256)
    per = tall // group if tall > group else 1
    steps = chans // tall
    sub = tall
    lanes = lax.broadcasted_iota(jnp.int32, (sub, width), 1)

    source = lax.broadcasted_iota(jnp.int32, (width, 2 * width), 0)
    target = lax.broadcasted_iota(jnp.int32, (width, 2 * width), 1)
    moves = (target == source + 1) & (target < width)
    moves = moves | (target == source + width + 2)
    shift = jnp.where(moves, 1.0, 0.0).astype(jnp.bfloat16)

    def feature(step, carry):
        block = lax.rem(me // per + step, steps)
        begin = pl.multiple_of(block * tall, tall)
        columns = cols_buf[:, pl.ds(begin, tall)].T
        parts = []
        for r in range(0, tall, sub):
            cols = columns[r : r + sub]
            here = pl.ds(begin + r, sub)
            made = []
            for s in range(3):
                x = s_ref[s, here, :].astype(jnp.float32)
                moved = jnp.dot(s_ref[s, here, :], shift, preferred_element_type=jnp.float32)
                one = jnp.where(lanes == 0, column(cols, 11 + 2 * s), moved[:, :width])
                two = jnp.where(lanes == 0, column(cols, 10 + 2 * s), moved[:, width:])
                two = jnp.where(lanes == 1, column(cols, 11 + 2 * s), two)
                made.append(
                    column(cols, 3 * s) * x
                    + column(cols, 3 * s + 1) * one
                    + column(cols, 3 * s + 2) * two
                )
            g = (made[1] * made[2]).astype(jnp.bfloat16)
            f0_buf[here, :] = made[0]
            mix_buf[here, :] = made[0] * (column(cols, 9) * g.astype(jnp.float32))
            if per == 1:
                gated[block, r : r + sub, :] = g
            else:
                parts.append(g.astype(jnp.float32))
        for q in range(per):
            peer = block * per + q
            if per > 1:
                begin = q * group % sub
                piece = parts[q * group // sub][begin : begin + group]
                gated[peer] = piece.astype(jnp.bfloat16)
            o = lax.rem(peer - me + n, n)

            @pl.when(o > 0)
            def _():
                send_x(0, o).start()

        return carry

    lax.fori_loop(1, steps + 1, feature, 0)
    for c in range(1, chunks):
        start_all(functools.partial(send_x, c), 1, n)
    own_x = pltpu.make_async_copy(gated.at[me], x_in.at[me], own_sem.at[1])
    own_x.start()
    own_h.wait()
    loads[3].wait()
    loads[4].wait()

    def drain(sem, count):
        some = s_ref.at[0, pl.ds(0, count)]
        pltpu.make_async_copy(some, some, sem).wait()

    drain(h_recv, (n - 1) * group)

    def filter_rows(r, carry):
        begin = pl.multiple_of(r * rows, rows)

        def load(a):
            return h_in[a, pl.ds(begin, rows), :]

        filt_buf[r] = forward(load, twist, mats, spec_buf, n, rows, width)
        return carry

    lax.fori_loop(0, group // rows, filter_rows, 0)
    own_x.wait()

    def conv_rows(r, carry):
        begin = pl.multiple_of(r * rows, rows)

        def load(a):
            return x_in[a, pl.ds(begin, rows), :]

        def store(a, value):
            y_out[a, pl.ds(begin, rows), :] = value

        fx = forward(load, twist, mats, spec_buf, n, rows, width)
        xr, xi = fx[:, :width], fx[:, width:]
        hr, hi = filt_buf[r, :, :width], filt_buf[r, :, width:]
        prod = jnp.concatenate([xr * hr - xi * hi, xr * hi + xi * hr], axis=1)
        backward(prod, store, twist, mats, spec_buf, n, rows, width)
        return carry

    own_y = []
    per_chunk = part // rows
    held, begins = ((1, chunks - 1) if chunks > 1 else (1,)), []
    for size in held:
        begins.append(sum(held[: len(begins)]))
    sent_parts = 0
    for c in range(chunks):
        drain(x_recv.at[c], (n - 1) * part)
        lax.fori_loop(c * per_chunk, (c + 1) * per_chunk, conv_rows, 0)
        ready = c + 1
        while sent_parts < len(held) and begins[sent_parts] + held[sent_parts] <= ready:
            q = sent_parts
            span = pl.ds(begins[q] * part, held[q] * part)
            start_all(lambda o, q=q, span=span: sent(y_out, y_in, y_send, y_recv.at[q], o, span), 1, n)
            own_y.append(pltpu.make_async_copy(y_out.at[me, span], y_in.at[me, span], own_sem.at[2 + q]))
            own_y[q].start()
            sent_parts += 1

    squares = jnp.zeros_like(sum_out)
    for q in range(len(held)):
        size = held[q] * part

        def mix(source):
            begin = pl.multiple_of(source * group + begins[q] * part, part)
            y = y_in[source, pl.ds(begins[q] * part, size), :].astype(jnp.float32)
            mixed = f0_buf[pl.ds(begin, size), :] * y + mix_buf[pl.ds(begin, size), :]
            out_ref[pl.ds(begin, size), :] = mixed
            return jnp.sum((mixed * mixed).reshape(size // 8, 8, width), axis=0)

        def finish(source, carry):
            return carry + mix(source)

        own_y[q].wait()
        drain(y_recv.at[q], (n - 1) * size)
        squares = lax.fori_loop(0, n, finish, squares, unroll=2)

    sum_out[...] = squares
    shared = []
    for o in range(1, cores):
        shared.append(
            pltpu.make_async_remote_copy(
                src_ref=sum_out, dst_ref=sum_in.at[core],
                send_sem=sum_send.at[o], recv_sem=sum_recv.at[o],
                device_id={"chan": lax.rem(core + o, cores)}, device_id_type=mesh_id,
            )
        )
        shared[-1].start()
    for sem in (h_send, x_send, y_send):
        drain(sem, (n - 1) * group)
    total = sum_out[...]
    for o in range(1, cores):
        shared[o - 1].wait()
        total = total + sum_in[lax.rem(core - o + cores, cores)]
    total = jnp.sum(total, axis=0, keepdims=True)
    inv_rms = lax.rsqrt(total / C + EPS)

    inv_ref[...] = inv_rms

    @pl.when(me < n - 1)
    def _():
        halo.wait_send()


CHUNKS = 4


def local(streams, feat_weights, skip_gain, filter_taps):
    n, cores = lax.axis_size("seq"), lax.axis_size("chan")
    chans, width = filter_taps.shape
    group = chans // n
    chunks = CHUNKS if group % (16 * CHUNKS) == 0 else 1
    rows = math.gcd(group // chunks, 32)
    twist, mats = tables(n, width)
    vmem = pl.BlockSpec(memory_space=pltpu.VMEM)
    dma = pltpu.SemaphoreType.DMA
    half = pltpu.VMEM((n, group, width), jnp.bfloat16)
    whole = pltpu.VMEM((chans, width), jnp.float32)
    mixed, inv = pl.pallas_call(
        functools.partial(fused_kernel, chunks),
        in_specs=[pl.BlockSpec(memory_space=pl.ANY)] * 6,
        out_specs=[vmem, vmem],
        out_shape=[pltpu.VMEM((chans, width), jnp.float32), pltpu.VMEM((1, width), jnp.float32)],
        scratch_shapes=[
            pltpu.VMEM(streams.shape, jnp.bfloat16),
            pltpu.VMEM((3, TAPS, chans), jnp.float32),
            pltpu.VMEM((1, chans), jnp.float32),
            pltpu.VMEM(twist.shape, jnp.float32),
            pltpu.VMEM(mats.shape, jnp.bfloat16),
            pltpu.VMEM((16, chans // 2), jnp.bfloat16),
            pltpu.VMEM((16, chans // 2), jnp.bfloat16),
            pltpu.VMEM((16, chans), jnp.float32),
            half, whole, whole, half, half, half, half,
            pltpu.VMEM((8, width), jnp.float32),
            pltpu.VMEM((cores, 8, width), jnp.float32),
            pltpu.VMEM((n + 1, rows, 2 * width), jnp.float32),
            pltpu.VMEM((group // rows, (n + 1) * rows, 2 * width), jnp.float32),
            dma((2,)),
            dma(()), dma(()), dma(()), dma((chunks,)),
            dma(()), dma((chunks,)),
            dma((cores,)), dma((cores,)), dma((2 + chunks,)), dma((5,)),
        ],
        compiler_params=pltpu.CompilerParams(
            collective_id=0, has_side_effects=True, vmem_limit_bytes=60 << 20
        ),
    )(
        streams, feat_weights.transpose(0, 2, 1), skip_gain[None, :],
        filter_taps.reshape(n, group, width), jnp.asarray(twist), jnp.asarray(mats),
    )
    return (mixed.astype(jnp.float32) * inv).astype(jnp.bfloat16)


def solution(mesh):
    placed = (P(None, "chan", "seq"), P(None, "chan", None), P("chan"), P("chan", "seq"))
    return jax.shard_map(
        local, mesh=mesh, in_specs=placed, out_specs=P("chan", "seq"), check_vma=False
    )
```

```python
import functools
import math

import jax
import jax.numpy as jnp
import numpy as np
from jax import lax
from jax.experimental import pallas as pl
from jax.experimental.pallas import tpu as pltpu
from jax.sharding import PartitionSpec as P

C = 4096
TAPS = 3
EPS = 1e-05


def add(a, b):
    if a is None:
        return b
    return a if b is None else a + b


def sub(a, b):
    if b is None:
        return a
    return -b if a is None else a - b


def times(pair, angle):
    re, im = pair
    c, s = math.cos(angle), math.sin(angle)
    if abs(s) < 1e-12 and c > 0:
        return pair
    if abs(c) < 1e-12:
        turned = (None if im is None else -im, re)
        return turned if s > 0 else (None if turned[0] is None else -turned[0], -re)
    if im is None:
        return (re * c, re * s)
    return (re * c - im * s, re * s + im * c)


def real_fft(xs, n):
    if n == 2:
        return [(xs[0], None), (xs[0], None)]
    even = real_fft(xs[0::2], n // 2)
    odd = real_fft(xs[1::2], n // 2)
    out = [None] * (n // 2 + 1)
    for k in range(n // 4 + 1):
        er, ei = even[k]
        tr, ti = times(odd[k], -2.0 * math.pi * k / n)
        out[k] = (add(er, tr), add(ei, ti))
        if n // 2 - k != k:
            out[n // 2 - k] = (sub(er, tr), sub(ti, ei))
    return out


def real_ifft(spec, n):
    if n == 2:
        return [spec[0][0] + spec[1][0]]
    even, odd = [], []
    for k in range(n // 4 + 1):
        ar, ai = spec[k]
        br, bi = spec[n // 2 - k]
        if n // 2 - k == k:
            er, ei, dr, di = ar + ar, None, None, add(ai, ai)
            even.append((er, ei))
            odd.append((-di if di is not None else None, None))
            continue
        even.append((ar + br, sub(ai, bi)))
        odd.append(times((ar - br, add(ai, bi)), 2.0 * math.pi * k / n))
    first = real_ifft(even, n // 2)
    second = real_ifft(odd, n // 2)
    out = []
    for a, b in zip(first, second):
        out += [a, b]
    return out


def tables(blocks, width):
    total = 2 * blocks * width
    k1 = np.arange(blocks + 1)[:, None]
    i = np.arange(width)[None, :]
    ang = 2.0 * np.pi * ((k1 * i) % total) / total
    twist = np.stack([np.cos(ang), np.sin(ang)]).astype(np.float32)[:, :, None, :]
    j = np.arange(width)
    ang = 2.0 * np.pi * ((j[:, None] * j[None, :]) % width) / width
    c, s = np.cos(ang), np.sin(ang)
    forward = np.block([[c, -s], [s, c]])
    inverse = np.block([[c, s], [-s, c]]) / total
    out = []
    for m in (forward, inverse):
        hi = m.astype(np.float32).astype(jnp.bfloat16)
        lo = (m - hi.astype(np.float64)).astype(np.float32).astype(jnp.bfloat16)
        out += [hi, lo]
    return twist, np.stack(out)


def split_dot(x, hi_w, lo_w):
    hi = x.astype(jnp.bfloat16)
    lo = (x - hi.astype(jnp.float32)).astype(jnp.bfloat16)
    dot = functools.partial(jnp.dot, preferred_element_type=jnp.float32)
    return dot(hi, hi_w) + (dot(lo, hi_w) + dot(hi, lo_w))


def forward(load, twist, mats, buf, blocks, rows, width):
    xs = [load(a).astype(jnp.float32) for a in range(blocks)]
    for k, (re, im) in enumerate(real_fft(xs, 2 * blocks)):
        tc, ts = twist[0, k], twist[1, k]
        if k == 0:
            new_re, new_im = re, jnp.zeros_like(re)
        elif im is None:
            new_re, new_im = re * tc, -(re * ts)
        else:
            new_re, new_im = re * tc + im * ts, im * tc - re * ts
        buf[k, :, :width] = new_re
        buf[k, :, width:] = new_im
    flat = (blocks + 1) * rows
    return split_dot(buf[...].reshape(flat, 2 * width), mats[0], mats[1])


def backward(prod, store, twist, mats, buf, blocks, rows, width):
    back = split_dot(prod, mats[2], mats[3])
    buf[...] = back.reshape(blocks + 1, rows, 2 * width)
    spec = []
    for k in range(blocks + 1):
        re, im = buf[k, :, :width], buf[k, :, width:]
        tc, ts = twist[0, k], twist[1, k]
        out_re = re if k == 0 else re * tc - im * ts
        out_im = None if k in (0, blocks) else re * ts + im * tc
        spec.append((out_re, out_im))
    for a, y in enumerate(real_ifft(spec, 2 * blocks)):
        store(a, y.astype(jnp.bfloat16))


def column(cols, j):
    return cols[:, j : j + 1]


def fused_kernel(
    chunks, s_hbm, w_hbm, g_hbm, h_ref, twist_hbm, mats_hbm, out_ref, inv_ref,
    s_ref, w_ref, g_ref, twist, mats, halo_out, halo_in, cols_buf, gated, f0_buf, mix_buf, h_in, x_in, y_out, y_in,
    sum_out, sum_in, spec_buf, filt_buf,
    halo_sem, h_send, h_recv, x_send, x_recv, y_send, y_recv, sum_send, sum_recv, own_sem,
    load_sem,
):
    n, group, width = gated.shape
    part = group // chunks
    rows = math.gcd(part, 32)
    chans = n * group
    cores = sum_in.shape[0]
    me = lax.axis_index("seq")
    core = lax.axis_index("chan")
    mesh_id = pl.DeviceIdType.MESH

    loads = [
        pltpu.make_async_copy(src, dst, load_sem.at[i])
        for i, (src, dst) in enumerate(
            [(s_hbm, s_ref), (w_hbm, w_ref), (g_hbm, g_ref), (twist_hbm, twist), (mats_hbm, mats)]
        )
    ]
    for copy in loads:
        copy.start()

    barrier = pltpu.get_barrier_semaphore()

    def greet(o, carry):
        peer = lax.rem(me + o, n)
        pl.semaphore_signal(barrier, inc=1, device_id={"seq": peer}, device_id_type=mesh_id)
        return carry

    lax.fori_loop(1, n, greet, 0)
    for o in range(1, cores):
        pl.semaphore_signal(
            barrier, inc=1, device_id={"chan": lax.rem(core + o, cores)}, device_id_type=mesh_id
        )

    def sent(src, dst, send, recv, o, span):
        peer = lax.rem(me + o, n)
        return pltpu.make_async_remote_copy(
            src_ref=src.at[peer, span], dst_ref=dst.at[me, span],
            send_sem=send, recv_sem=recv,
            device_id={"seq": peer}, device_id_type=mesh_id,
        )

    everything = pl.ds(0, group)

    def send_h(o):
        return sent(h_ref, h_in, h_send, h_recv, jnp.where(o <= n // 2, (1 - me // (n // 2)) * (n // 2) + lax.rem(me + o - 1, n // 2), me // (n // 2) * (n // 2) + lax.rem(me + o - n // 2, n // 2)) - me + n, everything)

    def send_x(c, o):
        return sent(gated, x_in, x_send, x_recv.at[c], o, pl.ds(c * part, part))

    def start_all(make, first, end):
        def body(o, carry):
            make(o).start()
            return carry

        lax.fori_loop(first, end, body, 0, unroll=True)

    row = lax.broadcasted_iota(jnp.int32, (16, width), 0)
    lane = lax.broadcasted_iota(jnp.int32, (16, width), 1)
    last = None
    loads[0].wait()
    for s in range(3):
        for top in range(2):
            first = 8 * top + 2 + 2 * s
            pick = ((row == first) & (lane == width - 2)) | ((row == first + 1) & (lane == width - 1))
            got = lax.dot_general(
                jnp.where(pick, 1.0, 0.0).astype(jnp.bfloat16),
                s_ref[s, top * chans // 2 : (top + 1) * chans // 2],
                (((1,), (1,)), ((), ())),
                preferred_element_type=jnp.float32,
            )
            last = got if last is None else last + got
    halo_out[...] = last.astype(jnp.bfloat16)

    halo = pltpu.make_async_remote_copy(
        src_ref=halo_out, dst_ref=halo_in, send_sem=halo_sem.at[0], recv_sem=halo_sem.at[1],
        device_id={"seq": lax.rem(me + 1, n)}, device_id_type=mesh_id,
    )
    pl.semaphore_wait(barrier, n - 1 + cores - 1)

    @pl.when(me < n - 1)
    def _():
        halo.start()

    start_all(send_h, 1, 1 + n // 2)
    start_all(send_h, 1 + n // 2, n)
    own_h = pltpu.make_async_copy(h_ref.at[me], h_in.at[me], own_sem.at[0])
    own_h.start()
    loads[1].wait()
    loads[2].wait()
    @pl.when(me > 0)
    def _():
        halo.wait_recv()

    for s in range(3):
        cols_buf[3 * s : 3 * s + 3, :] = w_ref[s]
    cols_buf[9:10, :] = g_ref[...]
    before = jnp.where(me > 0, halo_in[...].astype(jnp.float32), 0.0)
    cols_buf[10:16, : chans // 2] = before[2:8]
    cols_buf[10:16, chans // 2 :] = before[10:16]

    tall = math.gcd(chans, 256)
    per = tall // group if tall > group else 1
    steps = chans // tall
    sub = tall
    lanes = lax.broadcasted_iota(jnp.int32, (sub, width), 1)

    source = lax.broadcasted_iota(jnp.int32, (width, 2 * width), 0)
    target = lax.broadcasted_iota(jnp.int32, (width, 2 * width), 1)
    moves = (target == source + 1) & (target < width)
    moves = moves | (target == source + width + 2)
    shift = jnp.where(moves, 1.0, 0.0).astype(jnp.bfloat16)

    def feature(step, carry):
        block = lax.rem(me // per + step, steps)
        begin = pl.multiple_of(block * tall, tall)
        columns = cols_buf[:, pl.ds(begin, tall)].T
        parts = []
        for r in range(0, tall, sub):
            cols = columns[r : r + sub]
            here = pl.ds(begin + r, sub)
            made = []
            for s in range(3):
                x = s_ref[s, here, :].astype(jnp.float32)
                moved = jnp.dot(s_ref[s, here, :], shift, preferred_element_type=jnp.float32)
                one = jnp.where(lanes == 0, column(cols, 11 + 2 * s), moved[:, :width])
                two = jnp.where(lanes == 0, column(cols, 10 + 2 * s), moved[:, width:])
                two = jnp.where(lanes == 1, column(cols, 11 + 2 * s), two)
                made.append(
                    column(cols, 3 * s) * x
                    + column(cols, 3 * s + 1) * one
                    + column(cols, 3 * s + 2) * two
                )
            g = (made[1] * made[2]).astype(jnp.bfloat16)
            f0_buf[here, :] = made[0]
            mix_buf[here, :] = made[0] * (column(cols, 9) * g.astype(jnp.float32))
            if per == 1:
                gated[block, r : r + sub, :] = g
            else:
                parts.append(g.astype(jnp.float32))
        for q in range(per):
            peer = block * per + q
            if per > 1:
                begin = q * group % sub
                piece = parts[q * group // sub][begin : begin + group]
                gated[peer] = piece.astype(jnp.bfloat16)
            o = lax.rem(peer - me + n, n)

            @pl.when(o > 0)
            def _():
                send_x(0, o).start()

        return carry

    lax.fori_loop(1, steps + 1, feature, 0)
    for c in range(1, 1):
        start_all(functools.partial(send_x, c), 1, n)
    own_x = pltpu.make_async_copy(gated.at[me], x_in.at[me], own_sem.at[1])
    own_x.start()
    own_h.wait()
    loads[3].wait()
    loads[4].wait()

    def drain(sem, count):
        some = s_ref.at[0, pl.ds(0, count)]
        pltpu.make_async_copy(some, some, sem).wait()

    drain(h_recv, (n - 1) * group)

    def filter_rows(r, carry):
        begin = pl.multiple_of(r * rows, rows)

        def load(a):
            return h_in[a, pl.ds(begin, rows), :]

        filt_buf[r] = forward(load, twist, mats, spec_buf, n, rows, width)
        return carry

    for c in range(1, chunks):
        start_all(functools.partial(send_x, c), 1, n)
    lax.fori_loop(0, group // rows, filter_rows, 0)
    own_x.wait()

    def conv_rows(r, carry):
        begin = pl.multiple_of(r * rows, rows)

        def load(a):
            return x_in[a, pl.ds(begin, rows), :]

        def store(a, value):
            y_out[a, pl.ds(begin, rows), :] = value

        fx = forward(load, twist, mats, spec_buf, n, rows, width)
        xr, xi = fx[:, :width], fx[:, width:]
        hr, hi = filt_buf[r, :, :width], filt_buf[r, :, width:]
        prod = jnp.concatenate([xr * hr - xi * hi, xr * hi + xi * hr], axis=1)
        backward(prod, store, twist, mats, spec_buf, n, rows, width)
        return carry

    own_y = []
    per_chunk = part // rows
    held, begins = ((1, chunks - 1) if chunks > 1 else (1,)), []
    for size in held:
        begins.append(sum(held[: len(begins)]))
    sent_parts = 0
    for c in range(chunks):
        drain(x_recv.at[c], (n - 1) * part)
        lax.fori_loop(c * per_chunk, (c + 1) * per_chunk, conv_rows, 0)
        ready = c + 1
        while sent_parts < len(held) and begins[sent_parts] + held[sent_parts] <= ready:
            q = sent_parts
            span = pl.ds(begins[q] * part, held[q] * part)
            start_all(lambda o, q=q, span=span: sent(y_out, y_in, y_send, y_recv.at[q], o, span), 1, n)
            own_y.append(pltpu.make_async_copy(y_out.at[me, span], y_in.at[me, span], own_sem.at[2 + q]))
            own_y[q].start()
            sent_parts += 1

    squares = jnp.zeros_like(sum_out)
    for q in range(len(held)):
        size = held[q] * part

        def mix(source):
            begin = pl.multiple_of(source * group + begins[q] * part, part)
            y = y_in[source, pl.ds(begins[q] * part, size), :].astype(jnp.float32)
            mixed = f0_buf[pl.ds(begin, size), :] * y + mix_buf[pl.ds(begin, size), :]
            out_ref[pl.ds(begin, size), :] = mixed
            return jnp.sum((mixed * mixed).reshape(size // 8, 8, width), axis=0)

        def finish(source, carry):
            return carry + mix(source)

        own_y[q].wait()
        drain(y_recv.at[q], (n - 1) * size)
        squares = lax.fori_loop(0, n, finish, squares, unroll=2)

    sum_out[...] = squares
    shared = []
    for o in range(1, cores):
        shared.append(
            pltpu.make_async_remote_copy(
                src_ref=sum_out, dst_ref=sum_in.at[core],
                send_sem=sum_send.at[o], recv_sem=sum_recv.at[o],
                device_id={"chan": lax.rem(core + o, cores)}, device_id_type=mesh_id,
            )
        )
        shared[-1].start()
    for sem in (h_send, x_send, y_send):
        drain(sem, (n - 1) * group)
    total = sum_out[...]
    for o in range(1, cores):
        shared[o - 1].wait()
        total = total + sum_in[lax.rem(core - o + cores, cores)]
    total = jnp.sum(total, axis=0, keepdims=True)
    inv_rms = lax.rsqrt(total / C + EPS)

    inv_ref[...] = inv_rms

    @pl.when(me < n - 1)
    def _():
        halo.wait_send()


CHUNKS = 4


def local(streams, feat_weights, skip_gain, filter_taps):
    n, cores = lax.axis_size("seq"), lax.axis_size("chan")
    chans, width = filter_taps.shape
    group = chans // n
    chunks = CHUNKS if group % (16 * CHUNKS) == 0 else 1
    rows = math.gcd(group // chunks, 32)
    twist, mats = tables(n, width)
    vmem = pl.BlockSpec(memory_space=pltpu.VMEM)
    dma = pltpu.SemaphoreType.DMA
    half = pltpu.VMEM((n, group, width), jnp.bfloat16)
    whole = pltpu.VMEM((chans, width), jnp.float32)
    mixed, inv = pl.pallas_call(
        functools.partial(fused_kernel, chunks),
        in_specs=[pl.BlockSpec(memory_space=pl.ANY)] * 6,
        out_specs=[vmem, vmem],
        out_shape=[pltpu.VMEM((chans, width), jnp.float32), pltpu.VMEM((1, width), jnp.float32)],
        scratch_shapes=[
            pltpu.VMEM(streams.shape, jnp.bfloat16),
            pltpu.VMEM((3, TAPS, chans), jnp.float32),
            pltpu.VMEM((1, chans), jnp.float32),
            pltpu.VMEM(twist.shape, jnp.float32),
            pltpu.VMEM(mats.shape, jnp.bfloat16),
            pltpu.VMEM((16, chans // 2), jnp.bfloat16),
            pltpu.VMEM((16, chans // 2), jnp.bfloat16),
            pltpu.VMEM((16, chans), jnp.float32),
            half, whole, whole, half, half, half, half,
            pltpu.VMEM((8, width), jnp.float32),
            pltpu.VMEM((cores, 8, width), jnp.float32),
            pltpu.VMEM((n + 1, rows, 2 * width), jnp.float32),
            pltpu.VMEM((group // rows, (n + 1) * rows, 2 * width), jnp.float32),
            dma((2,)),
            dma(()), dma(()), dma(()), dma((chunks,)),
            dma(()), dma((chunks,)),
            dma((cores,)), dma((cores,)), dma((2 + chunks,)), dma((5,)),
        ],
        compiler_params=pltpu.CompilerParams(
            collective_id=0, has_side_effects=True, vmem_limit_bytes=60 << 20
        ),
    )(
        streams, feat_weights.transpose(0, 2, 1), skip_gain[None, :],
        filter_taps.reshape(n, group, width), jnp.asarray(twist), jnp.asarray(mats),
    )
    return (mixed.astype(jnp.float32) * inv).astype(jnp.bfloat16)


def solution(mesh):
    placed = (P(None, "chan", "seq"), P(None, "chan", None), P("chan"), P("chan", "seq"))
    return jax.shard_map(
        local, mesh=mesh, in_specs=placed, out_specs=P("chan", "seq"), check_vma=False
    )
```

```python
import functools
import math

import jax
import jax.numpy as jnp
import numpy as np
from jax import lax
from jax.experimental import pallas as pl
from jax.experimental.pallas import tpu as pltpu
from jax.sharding import PartitionSpec as P

C = 4096
TAPS = 3
EPS = 1e-05


def add(a, b):
    if a is None:
        return b
    return a if b is None else a + b


def sub(a, b):
    if b is None:
        return a
    return -b if a is None else a - b


def times(pair, angle):
    re, im = pair
    c, s = math.cos(angle), math.sin(angle)
    if abs(s) < 1e-12 and c > 0:
        return pair
    if abs(c) < 1e-12:
        turned = (None if im is None else -im, re)
        return turned if s > 0 else (None if turned[0] is None else -turned[0], -re)
    if im is None:
        return (re * c, re * s)
    return (re * c - im * s, re * s + im * c)


def real_fft(xs, n):
    if n == 2:
        return [(xs[0], None), (xs[0], None)]
    even = real_fft(xs[0::2], n // 2)
    odd = real_fft(xs[1::2], n // 2)
    out = [None] * (n // 2 + 1)
    for k in range(n // 4 + 1):
        er, ei = even[k]
        tr, ti = times(odd[k], -2.0 * math.pi * k / n)
        out[k] = (add(er, tr), add(ei, ti))
        if n // 2 - k != k:
            out[n // 2 - k] = (sub(er, tr), sub(ti, ei))
    return out


def real_ifft(spec, n):
    if n == 2:
        return [spec[0][0] + spec[1][0]]
    even, odd = [], []
    for k in range(n // 4 + 1):
        ar, ai = spec[k]
        br, bi = spec[n // 2 - k]
        if n // 2 - k == k:
            er, ei, dr, di = ar + ar, None, None, add(ai, ai)
            even.append((er, ei))
            odd.append((-di if di is not None else None, None))
            continue
        even.append((ar + br, sub(ai, bi)))
        odd.append(times((ar - br, add(ai, bi)), 2.0 * math.pi * k / n))
    first = real_ifft(even, n // 2)
    second = real_ifft(odd, n // 2)
    out = []
    for a, b in zip(first, second):
        out += [a, b]
    return out


def tables(blocks, width):
    total = 2 * blocks * width
    k1 = np.arange(blocks + 1)[:, None]
    i = np.arange(width)[None, :]
    ang = 2.0 * np.pi * ((k1 * i) % total) / total
    twist = np.stack([np.cos(ang), np.sin(ang)]).astype(np.float32)[:, :, None, :]
    j = np.arange(width)
    ang = 2.0 * np.pi * ((j[:, None] * j[None, :]) % width) / width
    c, s = np.cos(ang), np.sin(ang)
    forward = np.block([[c, -s], [s, c]])
    inverse = np.block([[c, s], [-s, c]]) / total
    out = []
    for m in (forward, inverse):
        hi = m.astype(np.float32).astype(jnp.bfloat16)
        lo = (m - hi.astype(np.float64)).astype(np.float32).astype(jnp.bfloat16)
        out += [hi, lo]
    return twist, np.stack(out)


def split_dot(x, hi_w, lo_w):
    hi = x.astype(jnp.bfloat16)
    lo = (x - hi.astype(jnp.float32)).astype(jnp.bfloat16)
    dot = functools.partial(jnp.dot, preferred_element_type=jnp.float32)
    return dot(hi, hi_w) + (dot(lo, hi_w) + dot(hi, lo_w))


def forward(load, twist, mats, buf, blocks, rows, width):
    xs = [load(a).astype(jnp.float32) for a in range(blocks)]
    for k, (re, im) in enumerate(real_fft(xs, 2 * blocks)):
        tc, ts = twist[0, k], twist[1, k]
        if k == 0:
            new_re, new_im = re, jnp.zeros_like(re)
        elif im is None:
            new_re, new_im = re * tc, -(re * ts)
        else:
            new_re, new_im = re * tc + im * ts, im * tc - re * ts
        buf[k, :, :width] = new_re
        buf[k, :, width:] = new_im
    flat = (blocks + 1) * rows
    return split_dot(buf[...].reshape(flat, 2 * width), mats[0], mats[1])


def backward(prod, store, twist, mats, buf, blocks, rows, width):
    back = split_dot(prod, mats[2], mats[3])
    buf[...] = back.reshape(blocks + 1, rows, 2 * width)
    spec = []
    for k in range(blocks + 1):
        re, im = buf[k, :, :width], buf[k, :, width:]
        tc, ts = twist[0, k], twist[1, k]
        out_re = re if k == 0 else re * tc - im * ts
        out_im = None if k in (0, blocks) else re * ts + im * tc
        spec.append((out_re, out_im))
    for a, y in enumerate(real_ifft(spec, 2 * blocks)):
        store(a, y.astype(jnp.bfloat16))


def column(cols, j):
    return cols[:, j : j + 1]


def fused_kernel(
    chunks, s_hbm, w_hbm, g_hbm, h_ref, twist_hbm, mats_hbm, out_ref, inv_ref,
    s_ref, w_ref, g_ref, twist, mats, halo_out, halo_in, cols_buf, gated, f0_buf, mix_buf, h_in, x_in, y_out, y_in,
    sum_out, sum_in, spec_buf, filt_buf,
    halo_sem, h_send, h_recv, x_send, x_recv, y_send, y_recv, sum_send, sum_recv, own_sem,
    load_sem,
):
    n, group, width = gated.shape
    part = group // chunks
    rows = math.gcd(part, 32)
    chans = n * group
    cores = sum_in.shape[0]
    me = lax.axis_index("seq")
    core = lax.axis_index("chan")
    mesh_id = pl.DeviceIdType.MESH

    loads = [
        pltpu.make_async_copy(src, dst, load_sem.at[i])
        for i, (src, dst) in enumerate(
            [(s_hbm, s_ref), (w_hbm, w_ref), (g_hbm, g_ref), (twist_hbm, twist), (mats_hbm, mats)]
        )
    ]
    for copy in loads:
        copy.start()

    barrier = pltpu.get_barrier_semaphore()

    def greet(o, carry):
        peer = lax.rem(me + o, n)
        pl.semaphore_signal(barrier, inc=1, device_id={"seq": peer}, device_id_type=mesh_id)
        return carry

    lax.fori_loop(1, n, greet, 0)
    for o in range(1, cores):
        pl.semaphore_signal(
            barrier, inc=1, device_id={"chan": lax.rem(core + o, cores)}, device_id_type=mesh_id
        )

    def sent(src, dst, send, recv, o, span):
        peer = lax.rem(me + o, n)
        return pltpu.make_async_remote_copy(
            src_ref=src.at[peer, span], dst_ref=dst.at[me, span],
            send_sem=send, recv_sem=recv,
            device_id={"seq": peer}, device_id_type=mesh_id,
        )

    everything = pl.ds(0, group)

    def send_h(o):
        return sent(h_ref, h_in, h_send, h_recv, jnp.where(o <= n // 2, (1 - me // (n // 2)) * (n // 2) + lax.rem(me + o - 1, n // 2), me // (n // 2) * (n // 2) + lax.rem(me + o - n // 2, n // 2)) - me + n, everything)

    def send_x(c, o):
        return sent(gated, x_in, x_send, x_recv.at[c], o if c == 0 else jnp.where(me >= n // 2, jnp.where(o <= n // 2, lax.rem(me + o - 1, n // 2), n // 2 + lax.rem(me + o - n // 2, n // 2)), lax.rem(me + o, n)) - me + n, pl.ds(c * part, part))

    def start_all(make, first, end):
        def body(o, carry):
            make(o).start()
            return carry

        lax.fori_loop(first, end, body, 0, unroll=True)

    row = lax.broadcasted_iota(jnp.int32, (16, width), 0)
    lane = lax.broadcasted_iota(jnp.int32, (16, width), 1)
    last = None
    loads[0].wait()
    for s in range(3):
        for top in range(2):
            first = 8 * top + 2 + 2 * s
            pick = ((row == first) & (lane == width - 2)) | ((row == first + 1) & (lane == width - 1))
            got = lax.dot_general(
                jnp.where(pick, 1.0, 0.0).astype(jnp.bfloat16),
                s_ref[s, top * chans // 2 : (top + 1) * chans // 2],
                (((1,), (1,)), ((), ())),
                preferred_element_type=jnp.float32,
            )
            last = got if last is None else last + got
    halo_out[...] = last.astype(jnp.bfloat16)

    halo = pltpu.make_async_remote_copy(
        src_ref=halo_out, dst_ref=halo_in, send_sem=halo_sem.at[0], recv_sem=halo_sem.at[1],
        device_id={"seq": lax.rem(me + 1, n)}, device_id_type=mesh_id,
    )
    pl.semaphore_wait(barrier, n - 1 + cores - 1)

    @pl.when(me < n - 1)
    def _():
        halo.start()

    start_all(send_h, 1, 1 + n // 2)
    start_all(send_h, 1 + n // 2, n)
    own_h = pltpu.make_async_copy(h_ref.at[me], h_in.at[me], own_sem.at[0])
    own_h.start()
    loads[1].wait()
    loads[2].wait()
    @pl.when(me > 0)
    def _():
        halo.wait_recv()

    for s in range(3):
        cols_buf[3 * s : 3 * s + 3, :] = w_ref[s]
    cols_buf[9:10, :] = g_ref[...]
    before = jnp.where(me > 0, halo_in[...].astype(jnp.float32), 0.0)
    cols_buf[10:16, : chans // 2] = before[2:8]
    cols_buf[10:16, chans // 2 :] = before[10:16]

    tall = math.gcd(chans, 256)
    per = tall // group if tall > group else 1
    steps = chans // tall
    sub = tall
    lanes = lax.broadcasted_iota(jnp.int32, (sub, width), 1)

    source = lax.broadcasted_iota(jnp.int32, (width, 2 * width), 0)
    target = lax.broadcasted_iota(jnp.int32, (width, 2 * width), 1)
    moves = (target == source + 1) & (target < width)
    moves = moves | (target == source + width + 2)
    shift = jnp.where(moves, 1.0, 0.0).astype(jnp.bfloat16)

    def feature(step, carry):
        block = lax.rem(me // per + step, steps)
        begin = pl.multiple_of(block * tall, tall)
        columns = cols_buf[:, pl.ds(begin, tall)].T
        parts = []
        for r in range(0, tall, sub):
            cols = columns[r : r + sub]
            here = pl.ds(begin + r, sub)
            made = []
            for s in range(3):
                x = s_ref[s, here, :].astype(jnp.float32)
                moved = jnp.dot(s_ref[s, here, :], shift, preferred_element_type=jnp.float32)
                one = jnp.where(lanes == 0, column(cols, 11 + 2 * s), moved[:, :width])
                two = jnp.where(lanes == 0, column(cols, 10 + 2 * s), moved[:, width:])
                two = jnp.where(lanes == 1, column(cols, 11 + 2 * s), two)
                made.append(
                    column(cols, 3 * s) * x
                    + column(cols, 3 * s + 1) * one
                    + column(cols, 3 * s + 2) * two
                )
            g = (made[1] * made[2]).astype(jnp.bfloat16)
            f0_buf[here, :] = made[0]
            mix_buf[here, :] = made[0] * (column(cols, 9) * g.astype(jnp.float32))
            if per == 1:
                gated[block, r : r + sub, :] = g
            else:
                parts.append(g.astype(jnp.float32))
        for q in range(per):
            peer = block * per + q
            if per > 1:
                begin = q * group % sub
                piece = parts[q * group // sub][begin : begin + group]
                gated[peer] = piece.astype(jnp.bfloat16)
            o = lax.rem(peer - me + n, n)

            @pl.when(o > 0)
            def _():
                send_x(0, o).start()

        return carry

    lax.fori_loop(1, steps + 1, feature, 0)
    for c in range(1, 1):
        start_all(functools.partial(send_x, c), 1, n)
    own_x = pltpu.make_async_copy(gated.at[me], x_in.at[me], own_sem.at[1])
    own_x.start()
    own_h.wait()
    loads[3].wait()
    loads[4].wait()

    def drain(sem, count):
        some = s_ref.at[0, pl.ds(0, count)]
        pltpu.make_async_copy(some, some, sem).wait()

    drain(h_recv, (n - 1) * group)

    def filter_rows(r, carry):
        begin = pl.multiple_of(r * rows, rows)

        def load(a):
            return h_in[a, pl.ds(begin, rows), :]

        filt_buf[r] = forward(load, twist, mats, spec_buf, n, rows, width)
        return carry

    for c in range(1, chunks):
        start_all(functools.partial(send_x, c), 1, n)
    lax.fori_loop(0, group // rows, filter_rows, 0)
    own_x.wait()

    def conv_rows(r, carry):
        begin = pl.multiple_of(r * rows, rows)

        def load(a):
            return x_in[a, pl.ds(begin, rows), :]

        def store(a, value):
            y_out[a, pl.ds(begin, rows), :] = value

        fx = forward(load, twist, mats, spec_buf, n, rows, width)
        xr, xi = fx[:, :width], fx[:, width:]
        hr, hi = filt_buf[r, :, :width], filt_buf[r, :, width:]
        prod = jnp.concatenate([xr * hr - xi * hi, xr * hi + xi * hr], axis=1)
        backward(prod, store, twist, mats, spec_buf, n, rows, width)
        return carry

    own_y = []
    per_chunk = part // rows
    held, begins = ((1, chunks - 1) if chunks > 1 else (1,)), []
    for size in held:
        begins.append(sum(held[: len(begins)]))
    sent_parts = 0
    for c in range(chunks):
        drain(x_recv.at[c], (n - 1) * part)
        lax.fori_loop(c * per_chunk, (c + 1) * per_chunk, conv_rows, 0)
        ready = c + 1
        while sent_parts < len(held) and begins[sent_parts] + held[sent_parts] <= ready:
            q = sent_parts
            span = pl.ds(begins[q] * part, held[q] * part)
            start_all(lambda o, q=q, span=span: sent(y_out, y_in, y_send, y_recv.at[q], o, span), 1, n)
            own_y.append(pltpu.make_async_copy(y_out.at[me, span], y_in.at[me, span], own_sem.at[2 + q]))
            own_y[q].start()
            sent_parts += 1

    squares = jnp.zeros_like(sum_out)
    for q in range(len(held)):
        size = held[q] * part

        def mix(source):
            begin = pl.multiple_of(source * group + begins[q] * part, part)
            y = y_in[source, pl.ds(begins[q] * part, size), :].astype(jnp.float32)
            mixed = f0_buf[pl.ds(begin, size), :] * y + mix_buf[pl.ds(begin, size), :]
            out_ref[pl.ds(begin, size), :] = mixed
            return jnp.sum((mixed * mixed).reshape(size // 8, 8, width), axis=0)

        def finish(source, carry):
            return carry + mix(source)

        own_y[q].wait()
        drain(y_recv.at[q], (n - 1) * size)
        squares = lax.fori_loop(0, n, finish, squares, unroll=2)

    sum_out[...] = squares
    shared = []
    for o in range(1, cores):
        shared.append(
            pltpu.make_async_remote_copy(
                src_ref=sum_out, dst_ref=sum_in.at[core],
                send_sem=sum_send.at[o], recv_sem=sum_recv.at[o],
                device_id={"chan": lax.rem(core + o, cores)}, device_id_type=mesh_id,
            )
        )
        shared[-1].start()
    for sem in (h_send, x_send, y_send):
        drain(sem, (n - 1) * group)
    total = sum_out[...]
    for o in range(1, cores):
        shared[o - 1].wait()
        total = total + sum_in[lax.rem(core - o + cores, cores)]
    total = jnp.sum(total, axis=0, keepdims=True)
    inv_rms = lax.rsqrt(total / C + EPS)

    inv_ref[...] = inv_rms

    @pl.when(me < n - 1)
    def _():
        halo.wait_send()


CHUNKS = 4


def local(streams, feat_weights, skip_gain, filter_taps):
    n, cores = lax.axis_size("seq"), lax.axis_size("chan")
    chans, width = filter_taps.shape
    group = chans // n
    chunks = CHUNKS if group % (16 * CHUNKS) == 0 else 1
    rows = math.gcd(group // chunks, 32)
    twist, mats = tables(n, width)
    vmem = pl.BlockSpec(memory_space=pltpu.VMEM)
    dma = pltpu.SemaphoreType.DMA
    half = pltpu.VMEM((n, group, width), jnp.bfloat16)
    whole = pltpu.VMEM((chans, width), jnp.float32)
    mixed, inv = pl.pallas_call(
        functools.partial(fused_kernel, chunks),
        in_specs=[pl.BlockSpec(memory_space=pl.ANY)] * 6,
        out_specs=[vmem, vmem],
        out_shape=[pltpu.VMEM((chans, width), jnp.float32), pltpu.VMEM((1, width), jnp.float32)],
        scratch_shapes=[
            pltpu.VMEM(streams.shape, jnp.bfloat16),
            pltpu.VMEM((3, TAPS, chans), jnp.float32),
            pltpu.VMEM((1, chans), jnp.float32),
            pltpu.VMEM(twist.shape, jnp.float32),
            pltpu.VMEM(mats.shape, jnp.bfloat16),
            pltpu.VMEM((16, chans // 2), jnp.bfloat16),
            pltpu.VMEM((16, chans // 2), jnp.bfloat16),
            pltpu.VMEM((16, chans), jnp.float32),
            half, whole, whole, half, half, half, half,
            pltpu.VMEM((8, width), jnp.float32),
            pltpu.VMEM((cores, 8, width), jnp.float32),
            pltpu.VMEM((n + 1, rows, 2 * width), jnp.float32),
            pltpu.VMEM((group // rows, (n + 1) * rows, 2 * width), jnp.float32),
            dma((2,)),
            dma(()), dma(()), dma(()), dma((chunks,)),
            dma(()), dma((chunks,)),
            dma((cores,)), dma((cores,)), dma((2 + chunks,)), dma((5,)),
        ],
        compiler_params=pltpu.CompilerParams(
            collective_id=0, has_side_effects=True, vmem_limit_bytes=60 << 20
        ),
    )(
        streams, feat_weights.transpose(0, 2, 1), skip_gain[None, :],
        filter_taps.reshape(n, group, width), jnp.asarray(twist), jnp.asarray(mats),
    )
    return (mixed.astype(jnp.float32) * inv).astype(jnp.bfloat16)


def solution(mesh):
    placed = (P(None, "chan", "seq"), P(None, "chan", None), P("chan"), P("chan", "seq"))
    return jax.shard_map(
        local, mesh=mesh, in_specs=placed, out_specs=P("chan", "seq"), check_vma=False
    )
```
